32 devices in a mesh: ctx: 8 (over y, x, core), ch: 4 (over z).
Axes of the slice: x: 2, y: 2, z: 4, core: 2. Of those that a mesh axis runs over, the one named last changes fastest.
Arguments:
- q_short: bfloat16 [1024, 8192], P('ctx', 'ch'), may hold values from -6 to 6
- k_short: bfloat16 [1024, 8192], P('ctx', 'ch'), may hold values from -6 to 6
- v_input: bfloat16 [1024, 8192], P('ctx', 'ch'), may hold values from -6 to 6
- q_long: bfloat16 [1024, 8192], P('ctx', 'ch'), may hold values from -6 to 6
- k_long: bfloat16 [1024, 8192], P('ctx', 'ch'), may hold values from -6 to 6
- short_filter: bfloat16 [128, 512], P(None, 'ch'), may hold values from -0.5 to 0.5
- decay_rates: float32 [512, 16], P('ch'), may hold values from 0.0001953125 to 0.04
- residues: float32 [512, 16], P('ch'), may hold values from -1.5 to 1.5
Outputs:
- mixed: bfloat16 [1024, 8192], P('ctx', 'ch')
The draws below stay inside these ranges and needn't reach their ends.
All inputs are finite; a program needn't handle non-finite values.
Results may differ from the reference program's by a relative error of at most 0.0065.
Values may be sent and summed in bfloat16 or wider, within the bound.
A program may use at most 64 MiB of HBM per device.

```python
import math
import jax
import jax.numpy as jnp
from jax import lax

D = 8192
TAPS = 128
ORDER = 16
SEQ = 1024
GROUPS = 512


def block_levels(key, extent, split, low, largest):
    factor_of = 1.0
    for dim, shards_of in split:
        heights = jax.random.uniform(jax.random.fold_in(jax.random.fold_in(key, 6), dim), (shards_of,), jnp.float32, low / len(split), largest / len(split))
        factor_of = factor_of * jnp.repeat(jnp.exp(heights), extent[dim] // shards_of).reshape((-1,) + (1,) * (len(extent) - 1 - dim))
    return factor_of


def bell_draw(own_key, extent, deviation, bound, cuts=(), held_as=jnp.bfloat16):
    factor_of = block_levels(own_key, extent, cuts, -0.22, 0.18) if cuts else 1.0
    values = jax.random.normal(own_key, extent, jnp.float32) * deviation * factor_of
    return jnp.minimum(jnp.maximum(values, -bound), bound).astype(held_as)


def setup_inputs(seed: int = 0) -> dict:
    splits = jax.random.split(jax.random.key(seed), 9)
    q_short = bell_draw(splits[0], (SEQ, D), 1.0, 6.0, ((0, 8), (1, 4)))
    k_short = bell_draw(splits[1], (SEQ, D), 1.0, 6.0, ((0, 8), (1, 4)))
    v_input = bell_draw(splits[2], (SEQ, D), 1.0, 6.0, ((0, 8), (1, 4)))
    q_long = bell_draw(splits[3], (SEQ, D), 1.0, 6.0, ((0, 8), (1, 4)))
    k_long = bell_draw(splits[4], (SEQ, D), 1.0, 6.0, ((0, 8), (1, 4)))
    short_filter = bell_draw(splits[5], (TAPS, GROUPS), TAPS ** -0.5, 0.5, ((1, 4),))
    decay_rates = jnp.clip(jnp.exp(math.log(0.04) - 5.322034 * jax.random.uniform(splits[6], (GROUPS, ORDER), jnp.float32) ** block_levels(splits[6], (GROUPS, ORDER), ((0, 4),), -0.2, 0.2)), 0.0001953125, 0.04)
    residues = bell_draw(splits[7], (GROUPS, ORDER), ORDER ** -0.5, 1.5, ((0, 4),), jnp.float32)
    return dict(q_short=q_short, k_short=k_short, v_input=v_input, q_long=q_long, k_long=k_long, short_filter=short_filter, decay_rates=decay_rates, residues=residues)


def mode_filter(positions, rates, weights):
    scaled = weights * jnp.sqrt(2.0 * rates)
    return lax.optimization_barrier(jnp.sum(scaled[None] * jnp.exp(-rates[None] * positions[:, None, None]), axis=-1))

def lag_matrix(column):
    reversed_col = jnp.concatenate([column[:1], column[:0:-1]], 0)
    tiled = jnp.tile(reversed_col, (128, 1))[:128 * 255]
    return tiled.reshape(128, 255, column.shape[1])[:, :128]

def short_tables(short_taps):
    blank = jnp.zeros_like(short_taps)
    near_table = lag_matrix(jnp.concatenate([short_taps, blank], 0))
    far_table = lag_matrix(jnp.concatenate([blank, short_taps], 0))
    return (near_table, far_table)

def reference(q_short, k_short, v_input, q_long, k_long, short_filter, decay_rates, residues):
    channels = q_short.shape[1]
    block_size = min(256, channels)
    blocks_total = channels // block_size
    group_block = block_size // 16
    positions = jnp.arange(SEQ).astype(jnp.float32)
    near_table, far_table = short_tables(short_filter.astype(jnp.float32))

    def by_block(array):
        return array.reshape(array.shape[0], blocks_total, block_size).transpose(1, 0, 2)

    def table_block(table):
        return table.reshape(128, 128, blocks_total, group_block).transpose(2, 0, 1, 3)
    stacked = (by_block(q_short), by_block(k_short), by_block(v_input), by_block(q_long), by_block(k_long), table_block(near_table), table_block(far_table), decay_rates.reshape(blocks_total, group_block, ORDER), residues.reshape(blocks_total, group_block, ORDER))
    highest = lax.Precision.HIGHEST

    def mixing(pieces):
        query_short, key_short, value_in, query_long, key_long, near_piece, far_piece, rates_piece, weights_piece = pieces
        u_short = lax.optimization_barrier((key_short.astype(jnp.float32) * value_in.astype(jnp.float32)).astype(jnp.bfloat16)).astype(jnp.float32)
        padded = jnp.concatenate([jnp.zeros((128, block_size), jnp.float32), u_short], 0)
        padded = padded.reshape(SEQ // 128 + 1, 128, group_block, 16)
        y_short = jnp.einsum('tsg,bsgk->btgk', near_piece, padded[1:], precision=highest)
        y_short = y_short + jnp.einsum('tsg,bsgk->btgk', far_piece, padded[:-1], precision=highest)
        y_short = y_short.reshape(SEQ, block_size)
        u_long = key_long.astype(jnp.float32) * query_short.astype(jnp.float32) * y_short
        u_long = lax.optimization_barrier(u_long.astype(jnp.bfloat16)).astype(jnp.float32)
        length = 2 * SEQ
        filt = mode_filter(positions, rates_piece, weights_piece)
        spectrum = jnp.repeat(jnp.fft.rfft(filt, n=length, axis=0), 16, axis=1)
        y_long = jnp.fft.irfft(jnp.fft.rfft(u_long, n=length, axis=0) * spectrum, n=length, axis=0)[:SEQ]
        y_long = lax.optimization_barrier(y_long.astype(jnp.bfloat16)).astype(jnp.float32)
        return (query_long.astype(jnp.float32) * y_long).astype(jnp.bfloat16)
    mixed = lax.map(mixing, stacked)
    return mixed.transpose(1, 0, 2).reshape(SEQ, channels)
```

```python
import functools

import jax
import jax.numpy as jnp
from jax import lax
from jax.experimental import pallas as pl
from jax.experimental.pallas import tpu as pltpu
from jax.sharding import PartitionSpec as P

MESH = pl.DeviceIdType.MESH
LANES = 128
F32 = jnp.float32
BF16 = jnp.bfloat16


def iota(shape, dim):
    return lax.broadcasted_iota(jnp.int32, shape, dim)


def split(x):
    hi = x.astype(BF16)
    return hi, (x - hi.astype(F32)).astype(BF16)


def kernel(
    n, chunks, q_short_in, k_short_in, v_input_in, q_long_in, k_long_in, taps, rates, weights, out,
    q_short, q_long, k_long, k_short, v_input, fetch_sem,
    ubuf, ulong, ynear, short_tab, long_tab, in_tab, out_tab, lam_rc, short_row, long_row, modes,
    state, psend, precv, halo_send, halo_recv, scan_send, scan_recv,
):
    me = lax.axis_index("ctx")
    tokens, ch = k_short_in.shape
    half = tokens // 2
    order, groups = rates.shape
    share = ch // groups
    per = LANES // share
    blocks = ch // LANES
    per_chunk = blocks // chunks
    width = per_chunk * LANES
    levels = n.bit_length() - 1

    barrier = pltpu.get_barrier_semaphore()
    for step in range(1, n):
        pl.semaphore_signal(
            barrier, inc=1, device_id={"ctx": lax.rem(me + step, n)}, device_id_type=MESH
        )

    fetches = [
        pltpu.make_async_copy(source, target, fetch_sem.at[i])
        for i, (source, target) in enumerate(
            (
                (q_short_in, q_short),
                (k_long_in, k_long),
                (q_long_in, q_long),
                (k_short_in, k_short),
                (v_input_in, v_input),
            )
        )
    ]
    for i in (3, 4):
        fetches[i].start()
    fetches[3].wait()
    fetches[4].wait()
    for i in (0, 1, 2):
        fetches[i].start()

    ubuf[pl.ds(tokens, tokens), :] = (k_short[...].astype(F32) * v_input[...].astype(F32)).astype(BF16)

    pl.semaphore_wait(barrier, n - 1)

    def halo(c):
        cols = pl.ds(c * width, width)
        return pltpu.make_async_remote_copy(
            src_ref=ubuf.at[pl.ds(tokens, tokens), cols],
            dst_ref=ubuf.at[pl.ds(0, tokens), cols],
            send_sem=halo_send.at[c],
            recv_sem=halo_recv.at[c],
            device_id={"ctx": lax.rem(me + 1, n)},
            device_id_type=MESH,
        )

    @pl.when(me < n - 1)
    def _():
        for c in range(chunks):
            halo(c).start()

    @pl.when(me == 0)
    def _():
        ubuf[pl.ds(0, tokens), :] = jnp.zeros((tokens, ch), BF16)

    ubuf[pl.ds(2 * tokens, half), :] = jnp.zeros((half, ch), BF16)
    ulong[pl.ds(0, half), :] = jnp.zeros((half, ch), BF16)

    rate = jnp.transpose(rates[...])
    scaled = jnp.transpose(weights[...]) * jnp.sqrt(2.0 * rate)
    reverse = lax.rem(tokens - iota((1, tokens), 1), tokens).astype(F32)
    total = jnp.zeros((groups, tokens), F32)
    for r in range(order):
        total = total + scaled[:, r : r + 1] * jnp.exp(-rate[:, r : r + 1] * reverse)
    long_row[...] = total
    flip = (lax.rem(iota((tokens, tokens), 0) + iota((tokens, tokens), 1), tokens) == 0).astype(BF16)
    taps_t = jnp.transpose(taps[...].astype(F32)).astype(BF16)
    short_row[...] = jnp.dot(taps_t, flip, preferred_element_type=F32)

    spread = (lax.rem(iota((order, LANES), 1), order) == iota((order, LANES), 0)).astype(F32)
    own = lax.rem(iota((groups, LANES), 0), per) == iota((groups, LANES), 1) // order

    def row_modes(x):
        wide = jnp.dot(x, spread, precision=lax.Precision.HIGHEST, preferred_element_type=F32)
        return jnp.where(own, wide, 0.0)

    rate_wide = row_modes(rate)
    modes[0] = jnp.sum(rate_wide.reshape(blocks, per, LANES), axis=1)
    modes[1] = jnp.sum(row_modes(scaled).reshape(blocks, per, LANES), axis=1)
    rate_tall = jnp.transpose(rate_wide)

    diag = iota((LANES, LANES), 0) // order == iota((LANES, LANES), 1) // share
    rows_half = iota((half, tokens), 0)
    lower = rows_half >= iota((half, tokens), 1)
    causal = rows_half + half >= iota((half, tokens), 1)

    def compact(x):
        return jnp.sum(jnp.where(diag, x, 0.0).reshape(per, order, LANES), axis=0)

    for b in range(blocks):
        in_block = iota((LANES, groups), 1) // per == b
        column = jnp.sum(jnp.where(in_block, rate_tall, 0.0), axis=1, keepdims=True)
        lam_rc[:, pl.ds(b * LANES, LANES)] = compact(jnp.broadcast_to(column, (LANES, LANES)))
        ahead = (tokens - iota((LANES, tokens), 1)).astype(F32)
        hi, lo = split(jnp.exp(-column * ahead))
        in_tab[b, :, pl.ds(0, tokens)] = hi
        in_tab[b, :, pl.ds(tokens, tokens)] = lo
        rows = iota((tokens, LANES), 0).astype(F32)
        hi, lo = split(modes[1, b : b + 1, :] * jnp.exp(-modes[0, b : b + 1, :] * rows))
        out_tab[b, :, pl.ds(0, LANES)] = hi
        out_tab[b, :, pl.ds(LANES, LANES)] = lo
        out_tab[b, :, pl.ds(2 * LANES, LANES)] = hi

    def tables(b, carry):
        at = pl.multiple_of(b * per, per)
        short8 = short_row[pl.ds(at, per), :]
        long8 = long_row[pl.ds(at, per), :]
        for g in range(per):
            turned = pltpu.roll(
                jnp.broadcast_to(short8[g : g + 1, :], (half, tokens)), 0, 1, stride=1, stride_axis=0
            )
            short_tab[b, pl.ds(g * half, half), pl.ds(0, tokens)] = jnp.where(lower, 0.0, turned).astype(BF16)
            short_tab[b, pl.ds(g * half, half), pl.ds(tokens, tokens)] = jnp.where(lower, turned, 0.0).astype(BF16)
            turned = pltpu.roll(
                jnp.broadcast_to(long8[g : g + 1, :], (half, tokens)), half, 1, stride=1, stride_axis=0
            )
            long_tab[b, :, pl.ds(g * tokens, tokens)] = jnp.where(causal, turned, 0.0).astype(BF16)
        return carry

    lax.fori_loop(0, blocks, tables, 0, unroll=2)
    fetches[0].wait()
    fetches[1].wait()

    lane_group = lax.rem(iota((half, 2 * LANES), 1), LANES) // share
    lane_group_tall = lax.rem(iota((tokens, 2 * LANES), 1), LANES) // share

    def windows(x):
        return jnp.concatenate([x[:, :LANES], x[:, LANES:]], 0)

    def short_block(b, carry):
        cols = pl.ds(pl.multiple_of(b * LANES, LANES), LANES)
        pair = jnp.concatenate([ubuf[pl.ds(0, 2 * tokens), cols], ubuf[pl.ds(half, 2 * tokens), cols]], 1)
        full = jnp.dot(short_tab[b], pair, preferred_element_type=F32)
        y = full[:half]
        for g in range(1, per):
            y = jnp.where(lane_group == g, full[g * half : (g + 1) * half], y)
        y = windows(y)
        u = (k_long[:, cols].astype(F32) * q_short[:, cols].astype(F32) * y).astype(BF16)
        ulong[pl.ds(half, tokens), cols] = u
        local = jnp.dot(in_tab[b], jnp.concatenate([u, u], 0), preferred_element_type=F32)
        psend[0, :, cols] = compact(local)
        return carry

    def long_block(b, carry):
        cols = pl.ds(pl.multiple_of(b * LANES, LANES), LANES)
        u = jnp.concatenate([ulong[pl.ds(0, tokens), cols], ulong[pl.ds(half, tokens), cols]], 1)
        wide = jnp.concatenate(
            [jnp.where(lane_group_tall == g, u, jnp.zeros_like(u)) for g in range(per)], 0
        )
        ynear[:, cols] = windows(jnp.dot(long_tab[b], wide, preferred_element_type=F32))
        return carry

    def final_block(b, carry):
        cols = pl.ds(pl.multiple_of(b * LANES, LANES), LANES)
        tall = jnp.where(diag, jnp.concatenate([state[:, cols]] * per, 0), 0.0)
        hi, lo = split(tall)
        far = jnp.dot(out_tab[b], jnp.concatenate([hi, hi, lo], 0), preferred_element_type=F32)
        y = (ynear[:, cols] + far).astype(BF16)
        out[:, cols] = (q_long[:, cols].astype(F32) * y.astype(F32)).astype(BF16)
        return carry

    def scan_copy(k, c, away):
        cols = pl.ds(c * width, width)
        return pltpu.make_async_remote_copy(
            src_ref=psend.at[k, :, cols],
            dst_ref=precv.at[k, :, cols],
            send_sem=scan_send.at[k, c, away],
            recv_sem=scan_recv.at[k, c],
            device_id={"ctx": lax.rem(me + 1 + away, n)},
            device_id_type=MESH,
        )

    def sends(k):
        return lax.rem(me, 2 << k) == (1 << k) - 1

    def scan_send_level(k, c):
        @pl.when(sends(k))
        def _():
            for away in range(1 << k):
                scan_copy(k, c, away).start()

    def scan_take_level(k, c):
        cols = pl.ds(c * width, width)

        @pl.when(lax.rem(me, 2 << k) >= (1 << k))
        def _():
            scan_copy(k, c, 0).wait_recv()
            distance = lax.rem(me, 1 << k) * tokens
            decay = jnp.exp(-lam_rc[:, cols] * distance.astype(F32))
            state[:, cols] = state[:, cols] + decay * precv[k, :, cols]

        if k + 1 < levels:
            decay = jnp.exp(-lam_rc[:, cols] * float(tokens))
            psend[k + 1, :, cols] = psend[0, :, cols] + decay * state[:, cols]

    def over(c, body):
        lax.fori_loop(c * per_chunk, (c + 1) * per_chunk, body, 0, unroll=True)

    def takes(stage):
        for k in range(levels):
            c = stage - 1 - k
            if 0 <= c < chunks:
                scan_take_level(k, c)
                if k + 1 < levels:
                    scan_send_level(k + 1, c)

    state[...] = jnp.zeros_like(state)
    for c in range(chunks):

        @pl.when(me > 0)
        def _():
            halo(c).wait_recv()

        over(c, short_block)
        scan_send_level(0, c)
        takes(c)
    fetches[2].wait()
    nears, ends = 0, 0
    for step in range(levels):
        stage = chunks + step
        goal = -(-chunks * (step + 1) // levels)
        while nears < goal:
            over(nears, long_block)
            nears += 1
        while ends < min(nears, stage - levels):
            over(ends, final_block)
            ends += 1
        takes(stage)
    for c in range(nears, chunks):
        over(c, long_block)
    for c in range(ends, chunks):
        over(c, final_block)

    @pl.when(me < n - 1)
    def _():
        for c in range(chunks):
            halo(c).wait_send()

    for k in range(levels):

        @pl.when(sends(k))
        def _():
            for c in range(chunks):
                for away in range(1 << k):
                    scan_copy(k, c, away).wait_send()


def on_device(n, *args):
    args = args[:6] + (args[6].T, args[7].T)
    args = tuple(pltpu.with_memory_space_constraint(a, pltpu.HBM) for a in args)
    q_short, taps, rates = args[0], args[5], args[6]
    tokens, ch = q_short.shape
    order, groups = rates.shape
    blocks = ch // LANES
    per = LANES * groups // ch
    chunks = max(c for c in (1, 2, 4) if blocks % c == 0)
    levels = n.bit_length() - 1
    dma = pltpu.SemaphoreType.DMA
    return pl.pallas_call(
        functools.partial(kernel, n, chunks),
        out_shape=jax.ShapeDtypeStruct((tokens, ch), BF16),
        in_specs=[pl.BlockSpec(memory_space=pltpu.HBM if i < 5 else pltpu.VMEM) for i in range(8)],
        out_specs=pl.BlockSpec(memory_space=pltpu.VMEM),
        scratch_shapes=[
            pltpu.VMEM((tokens, ch), BF16),
            pltpu.VMEM((tokens, ch), BF16),
            pltpu.VMEM((tokens, ch), BF16),
            pltpu.VMEM((tokens, ch), BF16),
            pltpu.VMEM((tokens, ch), BF16),
            dma((5,)),
            pltpu.VMEM((2 * tokens + tokens // 2, ch), BF16),
            pltpu.VMEM((tokens + tokens // 2, ch), BF16),
            pltpu.VMEM((tokens, ch), F32),
            pltpu.VMEM((blocks, per * tokens // 2, 2 * tokens), BF16),
            pltpu.VMEM((blocks, tokens // 2, per * tokens), BF16),
            pltpu.VMEM((blocks, LANES, 2 * tokens), BF16),
            pltpu.VMEM((blocks, tokens, 3 * LANES), BF16),
            pltpu.VMEM((order, ch), F32),
            pltpu.VMEM((groups, tokens), F32),
            pltpu.VMEM((groups, tokens), F32),
            pltpu.VMEM((2, blocks, LANES), F32),
            pltpu.VMEM((order, ch), F32),
            pltpu.VMEM((levels, order, ch), F32),
            pltpu.VMEM((levels, order, ch), F32),
            dma((chunks,)),
            dma((chunks,)),
            dma((levels, chunks, max(1, n // 2))),
            dma((levels, chunks)),
        ],
        compiler_params=pltpu.CompilerParams(
            collective_id=0, has_side_effects=True, vmem_limit_bytes=40 * 2**20
        ),
    )(*args)


def solution(mesh):
    in_specs = (P("ctx", "ch"),) * 5 + (P(None, "ch"), P("ch", None), P("ch", None))
    return jax.shard_map(
        functools.partial(on_device, mesh.shape["ctx"]),
        mesh=mesh,
        in_specs=in_specs,
        out_specs=P("ctx", "ch"),
        check_vma=False,
    )
```

```python
import functools
import math

import jax
import jax.numpy as jnp
from jax import lax
from jax.experimental import pallas as pl
from jax.experimental.pallas import tpu as pltpu
from jax.sharding import PartitionSpec as P

MESH = pl.DeviceIdType.MESH
LANES = 128
F32 = jnp.float32
BF16 = jnp.bfloat16
LOG2E = math.log2(math.e)
LAG = 3


def iota(shape, dim):
    return lax.broadcasted_iota(jnp.int32, shape, dim)


def split(x):
    hi = x.astype(BF16)
    return hi, (x - hi.astype(F32)).astype(BF16)


def kernel(
    n, chunks, q_short_in, k_short_in, v_input_in, q_long_in, k_long_in, taps_in, rates_in, weights_in, out,
    q_short, q_long, k_long, k_short, v_input, taps, rates, weights, fetch_sem, early_sem,
    ubuf, ulong, ynear, short_tab, long_tab, out_tab, masks, lam_rc, short_row, wide_sums, wide_pairs, modes,
    state, plocal, psend, precv, halo_send, halo_recv, swap_send, scan_send, scan_recv,
):
    me = lax.axis_index("ctx")
    tokens, ch = k_short.shape
    half = tokens // 2
    order, groups = rates.shape
    share = ch // groups
    per = LANES // share
    blocks = ch // LANES
    per_chunk = blocks // chunks
    width = per_chunk * LANES
    levels = n.bit_length() - 1
    parts = 2 if chunks % 2 == 0 else 1

    def early(i, part):
        source, target = ((k_short_in, k_short), (v_input_in, v_input))[i]
        cols = pl.ds(part * (ch // parts), ch // parts)
        return pltpu.make_async_copy(source.at[:, cols], target.at[:, cols], early_sem.at[i, part])

    fetches = [
        pltpu.make_async_copy(source, target, fetch_sem.at[i])
        for i, (source, target) in enumerate(
            (
                (taps_in, taps),
                (rates_in, rates),
                (weights_in, weights),
                (k_long_in, k_long),
                (q_short_in, q_short),
                (q_long_in, q_long),
            )
        )
    ]
    for part in range(parts):
        for i in range(2):
            early(i, part).start()

    barrier = pltpu.get_barrier_semaphore()
    for step in range(1, n):
        pl.semaphore_signal(
            barrier, inc=1, device_id={"ctx": lax.rem(me + step, n)}, device_id_type=MESH
        )
    for fetch in fetches:
        fetch.start()

    def halo(c, count=1):
        at = pl.ds(c * per_chunk, count * per_chunk)
        return pltpu.make_async_remote_copy(
            src_ref=ubuf.at[at, pl.ds(tokens, tokens), :],
            dst_ref=ubuf.at[at, pl.ds(0, tokens), :],
            send_sem=halo_send,
            recv_sem=halo_recv.at[c],
            device_id={"ctx": lax.rem(me + 1, n)},
            device_id_type=MESH,
        )

    for c in range(chunks):
        if c % (chunks // parts) == 0:
            for i in range(2):
                early(i, c // (chunks // parts)).wait()
        for b in range(c * per_chunk, (c + 1) * per_chunk):
            cols = pl.ds(b * LANES, LANES)
            ubuf[b, pl.ds(tokens, tokens), :] = (k_short[:, cols].astype(F32) * v_input[:, cols].astype(F32)).astype(BF16)
        if c == 0:
            pl.semaphore_wait(barrier, n - 1)

        @pl.when(me < n - 1)
        def _():
            halo(c).start()

    @pl.when(me == 0)
    def _():
        ubuf[:, pl.ds(0, tokens), :] = jnp.zeros((blocks, tokens, LANES), BF16)

    state[...] = jnp.zeros_like(state)

    for i in range(3):
        fetches[i].wait()
    rate = rates[...] * LOG2E
    scaled = weights[...] * jnp.sqrt(2.0 * rates[...])
    own = lax.rem(iota((groups, LANES), 0), per) == iota((groups, LANES), 1) // order

    def wide(x):
        x = jnp.transpose(jnp.concatenate([x, jnp.zeros((LANES - order, groups), F32)], 0))
        shift = order
        while shift < LANES:
            x = x + pltpu.roll(x, shift, 1)
            shift *= 2
        return jnp.where(own, x, 0.0)

    modes[0] = jnp.sum(wide(rate).reshape(blocks, per, LANES), axis=1)
    scaled_wide = wide(scaled)
    modes[1] = jnp.sum(scaled_wide.reshape(blocks, per, LANES), axis=1)
    wide_sums[...] = jnp.broadcast_to(jnp.sum(scaled_wide, axis=1, keepdims=True), (groups, LANES))
    hi = scaled_wide.astype(BF16).astype(F32)
    wide_pairs[...] = jnp.concatenate(
        [hi.reshape(blocks, per, LANES), (scaled_wide - hi).reshape(blocks, per, LANES)], 1
    ).astype(BF16)
    flip = (lax.rem(iota((tokens, tokens), 0) + iota((tokens, tokens), 1), tokens) == 0).astype(BF16)
    taps_t = jnp.transpose(taps[...].astype(F32)).astype(BF16)
    short_row[...] = jnp.dot(taps_t, flip, preferred_element_type=F32)

    ahead = -(tokens - iota((order, tokens), 1)).astype(F32)
    rows = -iota((tokens, LANES), 0).astype(F32)
    lane_block = iota((order, LANES), 1) // share
    first_lane = iota((per, tokens), 1) == 0
    rows_half = iota((half, tokens), 0)
    masks[0] = (rows_half < iota((half, tokens), 1)).astype(F32)
    masks[1] = (rows_half >= iota((half, tokens), 1)).astype(F32)
    masks[2] = (rows_half + half >= iota((half, tokens), 1)).astype(F32)
    diag = iota((LANES, LANES), 0) // order == iota((LANES, LANES), 1) // share

    def turn(row, shift):
        return pltpu.roll(jnp.broadcast_to(row, (half, tokens)), shift, 1, stride=1, stride_axis=0)

    def early_tables(b):
        lam = jnp.zeros((order, LANES), F32)
        for g in range(per):
            column = jnp.broadcast_to(rate[:, b * per + g : b * per + g + 1], (order, tokens))
            lam = jnp.where(lane_block == g, column, lam)
            hi, lo = split(jnp.exp2(column * ahead))
            long_tab[b, g, pl.ds(half, order), :] = hi
            long_tab[b, g, pl.ds(half + order, order), :] = lo
        lam_rc[:, pl.ds(b * LANES, LANES)] = lam
        for g in range(per):
            turned = turn(short_row[pl.ds(b * per + g, 1), :], 0)
            for side in range(2):
                short_tab[b, side, pl.ds(g * half, half), :] = (turned * masks[side]).astype(BF16)

    def late_tables(b):
        parts = [
            jnp.concatenate([long_tab[b, g, pl.ds(half + i * order, order), :] for g in range(per)], 0)
            for i in range(2)
        ]
        both = jnp.dot(wide_pairs[b], jnp.concatenate(parts, 1), preferred_element_type=F32)
        long8 = both[:per, :tokens] + both[:per, tokens:] + both[per:, :tokens]
        long8 = jnp.where(first_lane, wide_sums[pl.ds(b * per, per), :], long8)
        for g in range(per):
            long_tab[b, g, pl.ds(0, half), :] = (turn(long8[g : g + 1, :], half) * masks[2]).astype(BF16)
        out_tab[b] = (modes[1, pl.ds(b, 1), :] * jnp.exp2(modes[0, pl.ds(b, 1), :] * rows)).astype(BF16)

    lane_group = lax.rem(iota((half, 2 * LANES), 1), LANES) // share
    lane_group_tall = lax.rem(iota((tokens, 2 * LANES), 1), LANES) // share

    def windows(x):
        return jnp.concatenate([x[:, :LANES], x[:, LANES:]], 0)

    def short_blocks(bs):
        reach = tokens + half
        fulls = []
        for b in bs:
            pair = jnp.concatenate([ubuf[b, pl.ds(0, reach), :], ubuf[b, pl.ds(half, reach), :]], 1)
            table = jnp.concatenate([short_tab[b, 0], short_tab[b, 1][:, :half]], 1)
            fulls.append(jnp.dot(table, pair, preferred_element_type=F32))
        for b, full in zip(bs, fulls):
            cols = pl.ds(b * LANES, LANES)
            y = full[:half]
            for g in range(1, per):
                y = jnp.where(lane_group == g, full[g * half : (g + 1) * half], y)
            y = windows(y)
            ulong[b] = (k_long[:, cols].astype(F32) * q_short[:, cols].astype(F32) * y).astype(BF16)

    def long_blocks(bs):
        for b in bs:
            cols = pl.ds(b * LANES, LANES)
            u = ulong[b]
            u = jnp.concatenate([jnp.concatenate([jnp.zeros_like(u[:half]), u[:half]], 0), u], 1)
            tall = jnp.concatenate(
                [jnp.where(lane_group_tall == g, u, jnp.zeros_like(u)) for g in range(per)], 0
            )
            table = jnp.concatenate([long_tab[b, g] for g in range(per)], 1)
            full = jnp.dot(table, tall, preferred_element_type=F32)
            ynear[:, cols] = windows(full[:half])
            local = full[half : half + order, LANES:] + full[half + order :, LANES:]
            plocal[:, cols] = local
            psend[0, :, cols] = local.astype(BF16)

    def final_blocks(bs):
        for b in bs:
            cols = pl.ds(b * LANES, LANES)
            both = [jnp.concatenate([x] * per, 0) for x in split(state[:, cols])]
            tall = jnp.concatenate([jnp.where(diag, x, jnp.zeros_like(x)) for x in both], 0)
            table = out_tab[b]
            far = jnp.dot(jnp.concatenate([table, table], 1), tall, preferred_element_type=F32)
            y = (ynear[:, cols] + far).astype(BF16)
            out[:, cols] = (q_long[:, cols].astype(F32) * y.astype(F32)).astype(BF16)

    def members(c):
        return range(c * per_chunk, (c + 1) * per_chunk)

    def exchange(c, count=1):
        cols = pl.ds(c * width, count * width)
        return pltpu.make_async_remote_copy(
            src_ref=psend.at[0, :, cols],
            dst_ref=precv.at[0, :, cols],
            send_sem=swap_send,
            recv_sem=scan_recv.at[0, c],
            device_id={"ctx": me + 1 - 2 * lax.rem(me, 2)},
            device_id_type=MESH,
        )

    def scan_copy(k, c, away, count=1):
        cols = pl.ds(c * width, count * width)
        return pltpu.make_async_remote_copy(
            src_ref=psend.at[k, :, cols],
            dst_ref=precv.at[k, :, cols],
            send_sem=scan_send.at[away],
            recv_sem=scan_recv.at[k, c],
            device_id={"ctx": lax.rem(me + 2 + away, n)},
            device_id_type=MESH,
        )

    def sends(k):
        return lax.rem(me, 2 << k) == (1 << k) - 2

    def early_take(c):
        cols = pl.ds(c * width, width)
        for j in range(1, levels):

            @pl.when(sends(j))
            def _():
                exchange(c).wait_recv()
                lam = lam_rc[:, cols]
                total = jnp.exp2(-lam * float(tokens)) * plocal[:, cols] + precv[0, :, cols].astype(F32)
                if j > 1:
                    ahead_of = jnp.zeros((order, width), F32)
                    for k in range(1, j):
                        scan_copy(k, c, 0).wait_recv()
                        decay = jnp.exp2(-lam * float(((1 << k) - 2) * tokens))
                        ahead_of = ahead_of + decay * precv[k, :, cols].astype(F32)
                    state[:, cols] = ahead_of
                    total = total + jnp.exp2(-lam * float(2 * tokens)) * ahead_of
                psend[j, :, cols] = total.astype(BF16)
                for away in range(1 << j):
                    scan_copy(j, c, away).start()

    def late_take(c):
        cols = pl.ds(c * width, width)

        @pl.when(lax.rem(me, 2) == 1)
        def _():
            exchange(c).wait_recv()
            state[:, cols] = state[:, cols] + precv[0, :, cols].astype(F32)

        for k in range(1, levels):
            place = lax.rem(me, 2 << k)

            @pl.when(jnp.logical_and(place >= 1 << k, jnp.logical_or(place != (2 << k) - 2, me == n - 2)))
            def _():
                scan_copy(k, c, 0).wait_recv()
                distance = lax.rem(me, 1 << k) * tokens
                decay = jnp.exp2(-lam_rc[:, cols] * distance.astype(F32))
                state[:, cols] = state[:, cols] + decay * precv[k, :, cols].astype(F32)

    for b in members(0):
        early_tables(b)
    fetches[3].wait()
    fetches[4].wait()

    def after_long(c):
        @pl.when(me < n - 1)
        def _():
            exchange(c).start()

    for c in range(chunks):
        last = c == chunks - 1
        if c >= LAG:
            early_take(c - LAG)
        if last and c > 0:
            long_blocks(members(c - 1))
            after_long(c - 1)

        @pl.when(me > 0)
        def _():
            halo(c).wait_recv()

        short_blocks(members(c))
        for b in members(c):
            late_tables(b)
        if not last:
            for b in members(c + 1):
                early_tables(b)
            if c > 0:
                long_blocks(members(c - 1))
                after_long(c - 1)

    long_blocks(members(chunks - 1))
    after_long(chunks - 1)
    for c in range(max(0, chunks - LAG), chunks):
        early_take(c)
    fetches[5].wait()
    for c in range(chunks):
        late_take(c)
        final_blocks(members(c))

    @pl.when(me < n - 1)
    def _():
        halo(0, chunks).wait_send()
        exchange(0, chunks).wait_send()

    for k in range(1, levels):

        @pl.when(sends(k))
        def _():
            for away in range(1 << k):
                scan_copy(k, 0, away, chunks).wait_send()


def on_device(n, *args):
    args = args[:6] + (args[6].T, args[7].T)
    args = tuple(pltpu.with_memory_space_constraint(a, pltpu.HBM) for a in args)
    q_short, taps, rates = args[0], args[5], args[6]
    tokens, ch = q_short.shape
    order, groups = rates.shape
    blocks = ch // LANES
    per = LANES * groups // ch
    chunks = max(c for c in (1, 2, 4, 8) if blocks % c == 0)
    levels = n.bit_length() - 1
    dma = pltpu.SemaphoreType.DMA
    return pl.pallas_call(
        functools.partial(kernel, n, chunks),
        out_shape=jax.ShapeDtypeStruct((tokens, ch), BF16),
        in_specs=[pl.BlockSpec(memory_space=pltpu.HBM)] * 8,
        out_specs=pl.BlockSpec(memory_space=pltpu.VMEM),
        scratch_shapes=[
            pltpu.VMEM((tokens, ch), BF16),
            pltpu.VMEM((tokens, ch), BF16),
            pltpu.VMEM((tokens, ch), BF16),
            pltpu.VMEM((tokens, ch), BF16),
            pltpu.VMEM((tokens, ch), BF16),
            pltpu.VMEM(taps.shape, BF16),
            pltpu.VMEM((order, groups), F32),
            pltpu.VMEM((order, groups), F32),
            dma((6,)),
            dma((2, 2)),
            pltpu.VMEM((blocks, 2 * tokens, LANES), BF16),
            pltpu.VMEM((blocks, tokens, LANES), BF16),
            pltpu.VMEM((tokens, ch), F32),
            pltpu.VMEM((blocks, 2, per * tokens // 2, tokens), BF16),
            pltpu.VMEM((blocks, per, tokens // 2 + 2 * order, tokens), BF16),
            pltpu.VMEM((blocks, tokens, LANES), BF16),
            pltpu.VMEM((3, tokens // 2, tokens), F32),
            pltpu.VMEM((order, ch), F32),
            pltpu.VMEM((groups, tokens), F32),
            pltpu.VMEM((groups, LANES), F32),
            pltpu.VMEM((blocks, 2 * per, LANES), BF16),
            pltpu.VMEM((2, blocks, LANES), F32),
            pltpu.VMEM((order, ch), F32),
            pltpu.VMEM((order, ch), F32),
            pltpu.VMEM((levels, order, ch), BF16),
            pltpu.VMEM((levels, order, ch), BF16),
            dma,
            dma((chunks,)),
            dma,
            dma((max(1, n // 2),)),
            dma((levels, chunks)),
        ],
        compiler_params=pltpu.CompilerParams(
            collective_id=0, has_side_effects=True, vmem_limit_bytes=40 * 2**20
        ),
    )(*args)


def solution(mesh):
    in_specs = (P("ctx", "ch"),) * 5 + (P(None, "ch"), P("ch", None), P("ch", None))
    return jax.shard_map(
        functools.partial(on_device, mesh.shape["ctx"]),
        mesh=mesh,
        in_specs=in_specs,
        out_specs=P("ctx", "ch"),
        check_vma=False,
    )
```

```python
import functools
import math

import jax
import jax.numpy as jnp
from jax import lax
from jax.experimental import pallas as pl
from jax.experimental.pallas import tpu as pltpu
from jax.sharding import PartitionSpec as P

MESH = pl.DeviceIdType.MESH
LANES = 128
F32 = jnp.float32
BF16 = jnp.bfloat16
LOG2E = math.log2(math.e)
WINDOWS = 4
SPANS = 8
BLOCK = 8


def iota(shape, dim):
    return lax.broadcasted_iota(jnp.int32, shape, dim)


def split(x):
    hi = x.astype(BF16)
    return hi, (x - hi.astype(F32)).astype(BF16)


def kernel(
    n, chunks, q_short_in, k_short_in, v_input_in, q_long_in, k_long_in, taps_in, rates_in, weights_in, out,
    q_short, q_long, k_long, k_short, v_input, taps, rates, weights, fetch_sem, early_sem,
    ubuf, ulong, ynear, short_tab, long_tab, out_tab, masks, long_mask, lam_rc, short_row, modes,
    turned_modes, state, inner, plocal, psend, precv, ready, halo_send, halo_recv, swap_send, chip_send, relay_send, last_send, block_send, scan_recv,
):
    me = lax.axis_index("ctx")
    tokens, ch = k_short.shape
    size = tokens // WINDOWS
    tap_rows = tokens // SPANS
    order, groups = rates.shape
    share = ch // groups
    per = LANES // share
    blocks = ch // LANES
    per_chunk = blocks // chunks
    width = per_chunk * LANES
    levels = n.bit_length() - 1
    chips = min(n, BLOCK) // 2
    odd = lax.rem(me, 2)
    chip = lax.rem(me, 2 * chips) // 2
    first_level = (2 * chips).bit_length() - 1
    bounds = sorted({chunks // 2, chunks - chunks // 4, chunks} - {0})
    bounds = list(zip([0] + bounds[:-1], bounds))
    final = len(bounds) - 1
    parts = 2 if chunks % 2 == 0 else 1

    def early(i, part):
        source, target = ((k_short_in, k_short), (v_input_in, v_input))[i]
        cols = pl.ds(part * (ch // parts), ch // parts)
        return pltpu.make_async_copy(source.at[:, cols], target.at[:, cols], early_sem.at[i, part])

    fetches = [
        pltpu.make_async_copy(source, target, fetch_sem.at[i])
        for i, (source, target) in enumerate(
            (
                (taps_in, taps),
                (rates_in, rates),
                (weights_in, weights),
                (k_long_in, k_long),
                (q_short_in, q_short),
                (q_long_in, q_long),
            )
        )
    ]
    for part in range(parts):
        for i in range(2):
            early(i, part).start()

    barrier = pltpu.get_barrier_semaphore()

    def signal(semaphore, device):
        pl.semaphore_signal(
            semaphore, inc=1, device_id={"ctx": lax.rem(device + n, n)}, device_id_type=MESH
        )

    if n > BLOCK:
        for step in range(1, n):
            signal(barrier, me + step)
    else:
        signal(barrier, me + 1 - 2 * odd)

        @pl.when(jnp.logical_and(odd == 0, me > 0))
        def _():
            signal(barrier, me - 1)

        for step in range(1, chips):

            @pl.when(chip + step < chips)
            def _():
                for core in range(2):
                    signal(barrier, me - odd + 2 * step + core)

    for fetch in fetches:
        fetch.start()

    def halo(c, count=1):
        at = pl.ds(c * per_chunk, count * per_chunk)
        return pltpu.make_async_remote_copy(
            src_ref=ubuf.at[at, pl.ds(tokens, tokens), :],
            dst_ref=ubuf.at[at, pl.ds(0, tokens), :],
            send_sem=halo_send,
            recv_sem=halo_recv.at[c],
            device_id={"ctx": lax.rem(me + 1, n)},
            device_id_type=MESH,
        )

    for c in range(chunks):
        if c % (chunks // parts) == 0:
            for i in range(2):
                early(i, c // (chunks // parts)).wait()
        for b in range(c * per_chunk, (c + 1) * per_chunk):
            cols = pl.ds(b * LANES, LANES)
            ubuf[b, pl.ds(tokens, tokens), :] = (k_short[:, cols].astype(F32) * v_input[:, cols].astype(F32)).astype(BF16)
        if c == 0 and n > BLOCK:
            pl.semaphore_wait(barrier, n - 1)
        elif c == 0:
            ahead_of = jnp.logical_and(odd == 1, me < n - 1).astype(jnp.int32)
            pl.semaphore_wait(barrier, 1 + 2 * chip + ahead_of)

        @pl.when(me < n - 1)
        def _():
            halo(c).start()

    if n <= BLOCK:
        for step in range(1, chips):

            @pl.when(chip >= step)
            def _():
                for core in range(2):
                    signal(ready, me - odd - 2 * step + core)

    @pl.when(me == 0)
    def _():
        ubuf[:, pl.ds(0, tokens), :] = jnp.zeros((blocks, tokens, LANES), BF16)

    state[...] = jnp.zeros_like(state)

    for i in range(3):
        fetches[i].wait()
    rate = rates[...] * LOG2E
    scaled = weights[...] * jnp.sqrt(2.0 * rates[...])
    for i, x in enumerate((rate, scaled)):
        turned_modes[i] = jnp.transpose(jnp.concatenate([x, jnp.zeros((LANES - order, groups), F32)], 0))
    for i in range(2):
        row = turned_modes[i, pl.ds(0, blocks, stride=per), :]
        for g in range(1, per):
            row = row + pltpu.roll(turned_modes[i, pl.ds(g, blocks, stride=per), :], g * order, 1)
        modes[i] = row
    flip = (lax.rem(iota((tokens, tokens), 0) + iota((tokens, tokens), 1), tokens) == 0).astype(BF16)
    taps_t = jnp.transpose(taps[...].astype(F32)).astype(BF16)
    short_row[...] = jnp.dot(taps_t, flip, preferred_element_type=F32)

    lane = iota((order, LANES), 1)
    ahead = (lax.rem(lane, size) - size).astype(F32)
    first = lax.rem(lane, size) == 0
    first_row = lax.rem(iota((1, LANES), 1), size) == 0
    rows = -iota((size, LANES), 0).astype(F32)
    masks[0] = (iota((tap_rows, tokens), 0) < iota((tap_rows, tokens), 1)).astype(F32)
    masks[1] = (iota((tap_rows, tokens), 0) >= iota((tap_rows, tokens), 1)).astype(F32)
    long_mask[...] = (iota((size, LANES), 0) >= lax.rem(iota((size, LANES), 1), size)).astype(F32)
    def turn(row, count, shift):
        return pltpu.roll(jnp.broadcast_to(row, (count, LANES)), shift, 1, stride=1, stride_axis=0)

    def spread(x, start, count):
        at = start // LANES * LANES
        x = x[:, at : at + LANES]
        if x.shape[1] < LANES:
            x = jnp.concatenate([x, jnp.zeros((order, LANES - x.shape[1]), F32)], 1)
        return jnp.take_along_axis(x, start - at + lane // (LANES // count), axis=1)

    def make_tables(b):
        for g in range(per):
            turned = turn(short_row[pl.ds(b * per + g, 1), :], tap_rows, 0)
            for side in range(2):
                short_tab[b, side, pl.ds(g * tap_rows, tap_rows), :] = (turned * masks[side]).astype(BF16)
        for j in range(per // WINDOWS):
            start = b * per + j * WINDOWS
            table = jnp.exp2(spread(rate, start, WINDOWS) * ahead)
            hi, lo = split(table)
            long_tab[b, j, pl.ds(size, order), :] = hi
            long_tab[b, j, pl.ds(size + order, order), :] = lo
            row = jnp.sum(spread(scaled, start, WINDOWS) * jnp.where(first, 1.0, table), axis=0, keepdims=True)
            row = jnp.where(first_row, pltpu.roll(row, size, 1), row)
            long_tab[b, j, pl.ds(0, size), :] = (turn(row, size, LANES - size) * long_mask[...]).astype(BF16)
        lam_rc[:, pl.ds(b * LANES, LANES)] = spread(rate, b * per, per)
        out_tab[b] = (modes[1, pl.ds(b, 1), :] * jnp.exp2(modes[0, pl.ds(b, 1), :] * rows)).astype(BF16)

    lane_group = lax.rem(iota((tap_rows, SPANS * LANES), 1), LANES) // share
    lane_group_tall = lax.rem(iota((size, WINDOWS * LANES), 1), LANES) // share

    lane_group_order = lax.rem(iota((order, WINDOWS * LANES), 1), LANES) // share

    def stacked(x):
        return jnp.concatenate([x[:, i : i + LANES] for i in range(0, x.shape[1], LANES)], 0)

    def beside(x):
        return jnp.concatenate([x[i : i + size] for i in range(0, tokens, size)], 1)

    def short_blocks(bs):
        reach = tokens + tap_rows
        fulls = []
        for b in bs:
            spans = jnp.concatenate([ubuf[b, pl.ds(w * tap_rows, reach), :] for w in range(SPANS)], 1)
            table = jnp.concatenate([short_tab[b, 0], short_tab[b, 1][:, :tap_rows]], 1)
            fulls.append(jnp.dot(table, spans, preferred_element_type=F32))
        for b, full in zip(bs, fulls):
            cols = pl.ds(b * LANES, LANES)
            y = full[:tap_rows]
            for g in range(1, per):
                y = jnp.where(lane_group == g, full[g * tap_rows : (g + 1) * tap_rows], y)
            y = stacked(y)
            ulong[b] = (k_long[:, cols].astype(F32) * q_short[:, cols].astype(F32) * y).astype(BF16)

    def pieces(x):
        return [x[:, i : i + LANES] for i in range(0, x.shape[1], LANES)]

    def long_blocks(bs):
        for b in bs:
            cols = pl.ds(b * LANES, LANES)
            u = beside(ulong[b])
            tall = jnp.concatenate(
                [jnp.where(lane_group_tall == g, u, jnp.zeros_like(u)) for g in range(per)], 0
            )
            table = jnp.concatenate([long_tab[b, j] for j in range(per // WINDOWS)], 1)
            full = jnp.dot(table, tall, preferred_element_type=F32)
            ynear[b] = full[:size]
            local = full[size : size + order] + full[size + order :]
            inner[b] = local
            decay = jnp.exp2(-lam_rc[:, cols] * float(size))
            total = local[:, :LANES]
            for piece in pieces(local)[1:]:
                total = decay * total + piece
            plocal[:, cols] = total
            psend[0, :, cols] = total.astype(BF16)

    def final_blocks(bs):
        for b in bs:
            cols = pl.ds(b * LANES, LANES)
            decay = jnp.exp2(-lam_rc[:, cols] * float(size))
            starts = [state[:, cols]]
            for piece in pieces(inner[b])[:-1]:
                starts.append(decay * starts[-1] + piece)
            tall = jnp.concatenate(
                [
                    jnp.where(lane_group_order == g, x, jnp.zeros_like(x))
                    for x in split(jnp.concatenate(starts, 1))
                    for g in range(per)
                ],
                0,
            )
            table = out_tab[b]
            far = jnp.dot(jnp.concatenate([table, table], 1), tall, preferred_element_type=F32)
            y = stacked(ynear[b] + far).astype(BF16)
            out[:, cols] = (q_long[:, cols].astype(F32) * y.astype(F32)).astype(BF16)

    def members(c):
        return range(c * per_chunk, (c + 1) * per_chunk)

    def columns(g, to=None):
        start, stop = bounds[g][0] * width, bounds[g if to is None else to][1] * width
        return pl.ds(start, stop - start)

    def send(source, target, g, send_sem, device, to=None):
        cols = columns(g, to)
        return pltpu.make_async_remote_copy(
            src_ref=psend.at[source, :, cols],
            dst_ref=precv.at[target, :, cols],
            send_sem=send_sem,
            recv_sem=scan_recv.at[target, g],
            device_id={"ctx": lax.rem(device, n)},
            device_id_type=MESH,
        )

    def swap(g, to=None):
        return send(0, 0, g, swap_send, me + 1 - 2 * odd, to)

    def chip_copy(g, step, to=None):
        return send(1, 1 + chip, g, chip_send.at[step - 1], me + 2 * step - 1, to)

    def relay(g, to=None):
        return send(2, chips, g, relay_send, me + 1, to)

    def last_copy(step, core):
        return send(1, 1 + chip, final, last_send.at[step - 1, core], me + 2 * step + core)

    def block_copy(k, g, away, to=None):
        return send(3, chips + 1 + k - first_level, g, block_send.at[away], me + 2 + away, to)

    def arrived(slot, g):
        send(0, slot, g, swap_send, me + 1).wait_recv()
        return precv[slot, :, columns(g)].astype(F32)

    def decayed(g, distance):
        return jnp.exp2(-lam_rc[:, columns(g)] * distance)

    def in_later_chip(step):
        return chip + step < chips

    def group_done(g):
        both_ways = jnp.logical_or(odd == 0, chip < chips - 1) if n <= BLOCK else odd >= 0
        one_way = odd == 0 if n <= BLOCK else jnp.logical_or(odd == 0, chip == chips - 1)

        @pl.when(both_ways if g == final else one_way)
        def _():
            swap(g).start()

    def odd_send(g):
        @pl.when(jnp.logical_and(odd == 1, chip < chips - 1))
        def _():
            total = decayed(g, float(tokens)) * arrived(0, g) + plocal[:, columns(g)]
            psend[1, :, columns(g)] = total.astype(BF16)
            for step in range(1, chips):

                @pl.when(in_later_chip(step))
                def _():
                    chip_copy(g, step).start()

    def even_send_last():
        @pl.when(jnp.logical_and(odd == 0, chip < chips - 1))
        def _():
            total = decayed(final, float(tokens)) * plocal[:, columns(final)] + arrived(0, final)
            psend[1, :, columns(final)] = total.astype(BF16)
            for step in range(1, chips):

                @pl.when(in_later_chip(step))
                def _():
                    for core in range(2):
                        last_copy(step, core).start()

    def take_chips(g, cores):
        cols = columns(g)
        for source in range(chips - 1):

            @pl.when(jnp.logical_and(chip > source, odd < cores))
            def _():
                distance = ((chip - source - 1) * 2 + odd) * tokens
                state[:, cols] = state[:, cols] + decayed(g, distance.astype(F32)) * arrived(1 + source, g)

    def take(g):
        cols = columns(g)
        take_chips(g, 1 if g < final else 2)
        if g < final:

            @pl.when(jnp.logical_and(odd == 0, chip > 0))
            def _():
                psend[2, :, cols] = state[:, cols].astype(BF16)
                relay(g).start()

            @pl.when(jnp.logical_and(odd == 1, chip > 0))
            def _():
                state[:, cols] = decayed(g, float(tokens)) * arrived(chips, g)

        @pl.when(jnp.logical_and(odd == 1, jnp.logical_or(chip == chips - 1, g == final)))
        def _():
            send(0, 0, g, swap_send, me + 1).wait_recv()

        @pl.when(odd == 1)
        def _():
            state[:, cols] = state[:, cols] + precv[0, :, cols].astype(F32)

        if n > BLOCK:
            last_even = jnp.logical_and(odd == 0, chip == chips - 1)

            @pl.when(last_even)
            def _():
                send(0, 0, g, swap_send, me + 1).wait_recv()

            for k in range(first_level, levels):

                @pl.when(lax.rem(me, 2 << k) >= 1 << k)
                def _():
                    distance = lax.rem(me, 1 << k) * tokens
                    slot = chips + 1 + k - first_level
                    state[:, cols] = state[:, cols] + decayed(g, distance.astype(F32)) * arrived(slot, g)

                @pl.when(sends(k))
                def _():
                    total = decayed(g, float(2 * tokens)) * state[:, cols]
                    total = total + decayed(g, float(tokens)) * plocal[:, cols]
                    psend[3, :, cols] = (total + precv[0, :, cols].astype(F32)).astype(BF16)
                    for away in range(1 << k):
                        block_copy(k, g, away).start()

    def sends(k):
        return lax.rem(me, 2 << k) == (1 << k) - 2

    for b in members(0):
        make_tables(b)
    fetches[3].wait()
    fetches[4].wait()

    def after_long(c):
        for g, (_, stop) in enumerate(bounds):
            if stop == c + 1:
                group_done(g)

    for c in range(chunks):
        last = c == chunks - 1
        if last and c > 0:
            long_blocks(members(c - 1))
            after_long(c - 1)

        @pl.when(me > 0)
        def _():
            halo(c).wait_recv()

        short_blocks(members(c))
        if not last:
            for b in members(c + 1):
                make_tables(b)
            if c > 0:
                long_blocks(members(c - 1))
                after_long(c - 1)

    long_blocks(members(chunks - 1))
    after_long(chunks - 1)
    if n <= BLOCK:

        @pl.when(chip < chips - 1)
        def _():
            pl.semaphore_wait(ready, 2 * (chips - 1 - chip))

    even_send_last()
    for g in range(final):
        odd_send(g)
    fetches[5].wait()
    for g in range(final + 1):
        take(g)
        for c in range(*bounds[g]):
            final_blocks(members(c))

    @pl.when(me < n - 1)
    def _():
        halo(0, chunks).wait_send()

    @pl.when(odd == 0)
    def _():
        swap(0, final).wait_send()

    if n > BLOCK:

        @pl.when(jnp.logical_and(odd == 1, chip == chips - 1))
        def _():
            swap(0, final).wait_send()

    @pl.when(jnp.logical_and(odd == 1, chip < chips - 1))
    def _():
        swap(final).wait_send()

    for step in range(1, chips):

        @pl.when(in_later_chip(step))
        def _():
            if final > 0:

                @pl.when(odd == 1)
                def _():
                    chip_copy(0, step, final - 1).wait_send()

            @pl.when(odd == 0)
            def _():
                for core in range(2):
                    last_copy(step, core).wait_send()

    if final > 0:

        @pl.when(jnp.logical_and(odd == 0, chip > 0))
        def _():
            relay(0, final - 1).wait_send()

    for k in range(first_level, levels):

        @pl.when(sends(k))
        def _():
            for away in range(1 << k):
                block_copy(k, 0, away, final).wait_send()


def on_device(n, *args):
    args = args[:6] + (args[6].T, args[7].T)
    args = tuple(pltpu.with_memory_space_constraint(a, pltpu.HBM) for a in args)
    q_short, taps, rates = args[0], args[5], args[6]
    tokens, ch = q_short.shape
    order, groups = rates.shape
    blocks = ch // LANES
    per = LANES * groups // ch
    chunks = max(c for c in (1, 2, 4, 8) if blocks % c == 0)
    levels = n.bit_length() - 1
    chips = min(n, BLOCK) // 2
    above = max(0, levels - chips.bit_length())
    dma = pltpu.SemaphoreType.DMA
    return pl.pallas_call(
        functools.partial(kernel, n, chunks),
        out_shape=jax.ShapeDtypeStruct((tokens, ch), BF16),
        in_specs=[pl.BlockSpec(memory_space=pltpu.HBM)] * 8,
        out_specs=pl.BlockSpec(memory_space=pltpu.VMEM),
        scratch_shapes=[
            pltpu.VMEM((tokens, ch), BF16),
            pltpu.VMEM((tokens, ch), BF16),
            pltpu.VMEM((tokens, ch), BF16),
            pltpu.VMEM((tokens, ch), BF16),
            pltpu.VMEM((tokens, ch), BF16),
            pltpu.VMEM(taps.shape, BF16),
            pltpu.VMEM((order, groups), F32),
            pltpu.VMEM((order, groups), F32),
            dma((6,)),
            dma((2, 2)),
            pltpu.VMEM((blocks, 2 * tokens, LANES), BF16),
            pltpu.VMEM((blocks, tokens, LANES), BF16),
            pltpu.VMEM((blocks, tokens // WINDOWS, WINDOWS * LANES), F32),
            pltpu.VMEM((blocks, 2, per * tokens // SPANS, tokens), BF16),
            pltpu.VMEM((blocks, per // WINDOWS, tokens // WINDOWS + 2 * order, LANES), BF16),
            pltpu.VMEM((blocks, tokens // WINDOWS, LANES), BF16),
            pltpu.VMEM((2, tokens // SPANS, tokens), F32),
            pltpu.VMEM((tokens // WINDOWS, LANES), F32),
            pltpu.VMEM((order, ch), F32),
            pltpu.VMEM((groups, tokens), F32),
            pltpu.VMEM((2, blocks, LANES), F32),
            pltpu.VMEM((2, groups, LANES), F32),
            pltpu.VMEM((order, ch), F32),
            pltpu.VMEM((blocks, order, WINDOWS * LANES), F32),
            pltpu.VMEM((order, ch), F32),
            pltpu.VMEM((4 if above else 3, order, ch), BF16),
            pltpu.VMEM((chips + 1 + above, order, ch), BF16),
            pltpu.SemaphoreType.REGULAR,
            dma,
            dma((chunks,)),
            dma,
            dma((max(1, chips - 1),)),
            dma,
            dma((max(1, chips - 1), 2)),
            dma((max(1, n // 2 if above else 1),)),
            dma((chips + 1 + above, 3)),
        ],
        compiler_params=pltpu.CompilerParams(
            collective_id=0, has_side_effects=True, vmem_limit_bytes=40 * 2**20
        ),
    )(*args)


def solution(mesh):
    in_specs = (P("ctx", "ch"),) * 5 + (P(None, "ch"), P("ch", None), P("ch", None))
    return jax.shard_map(
        functools.partial(on_device, mesh.shape["ctx"]),
        mesh=mesh,
        in_specs=in_specs,
        out_specs=P("ctx", "ch"),
        check_vma=False,
    )
```

```python
import functools
import math

import jax
import jax.numpy as jnp
from jax import lax
from jax.experimental import pallas as pl
from jax.experimental.pallas import tpu as pltpu
from jax.sharding import PartitionSpec as P

MESH = pl.DeviceIdType.MESH
LANES = 128
F32 = jnp.float32
BF16 = jnp.bfloat16
LOG2E = math.log2(math.e)
WINDOWS = 4
SPANS = 8
BLOCK = 8


def iota(shape, dim):
    return lax.broadcasted_iota(jnp.int32, shape, dim)


def split(x):
    hi = x.astype(BF16)
    return hi, (x - hi.astype(F32)).astype(BF16)


def kernel(
    n, chunks, q_short_in, k_short_in, v_input_in, q_long_in, k_long_in, taps_in, rates_in, weights_in, out,
    q_short, q_long, k_long, k_short, v_input, taps, rates, weights, fetch_sem, early_sem,
    ubuf, ulong, ynear, short_tab, long_tab, out_tab, masks, long_mask, lam_rc, short_row, modes,
    turned_modes, state, inner, plocal, psend, precv, ready, halo_send, halo_recv, swap_send, chip_send, forward_send, merged_send, block_send, scan_recv,
):
    me = lax.axis_index("ctx")
    tokens, ch = k_short.shape
    size = tokens // WINDOWS
    tap_rows = tokens // SPANS
    order, groups = rates.shape
    share = ch // groups
    per = LANES // share
    blocks = ch // LANES
    per_chunk = blocks // chunks
    width = per_chunk * LANES
    levels = n.bit_length() - 1
    chips = min(n, BLOCK) // 2
    odd = lax.rem(me, 2)
    chip = lax.rem(me, 2 * chips) // 2
    first_level = (2 * chips).bit_length() - 1
    bounds = sorted({chunks // 2, chunks - 1, chunks} - {0})
    bounds = list(zip([0] + bounds[:-1], bounds))
    final = len(bounds) - 1
    parts = 2 if chunks % 2 == 0 else 1

    def early(i, part):
        source, target = ((k_short_in, k_short), (v_input_in, v_input))[i]
        cols = pl.ds(part * (ch // parts), ch // parts)
        return pltpu.make_async_copy(source.at[:, cols], target.at[:, cols], early_sem.at[i, part])

    fetches = [
        pltpu.make_async_copy(source, target, fetch_sem.at[i])
        for i, (source, target) in enumerate(
            (
                (taps_in, taps),
                (rates_in, rates),
                (weights_in, weights),
                (k_long_in, k_long),
                (q_short_in, q_short),
                (q_long_in, q_long),
            )
        )
    ]
    barrier = pltpu.get_barrier_semaphore()

    def signal(semaphore, device):
        pl.semaphore_signal(
            semaphore, inc=1, device_id={"ctx": lax.rem(device + n, n)}, device_id_type=MESH
        )

    if n > BLOCK:
        for part in range(parts):
            for i in range(2):
                early(i, part).start()
        for step in range(1, n):
            signal(barrier, me + step)
    else:

        @pl.when(jnp.logical_and(odd == 0, me > 0))
        def _():
            signal(barrier, me - 1)

        for part in range(parts):
            for i in range(2):
                early(i, part).start()
        signal(barrier, me + 1 - 2 * odd)
        for step in range(1, chips):

            @pl.when(chip + step < chips)
            def _():
                for core in range(2):
                    signal(barrier, me - odd + 2 * step + core)

    for fetch in fetches:
        fetch.start()

    def halo(c, count=1):
        at = pl.ds(c * per_chunk, count * per_chunk)
        return pltpu.make_async_remote_copy(
            src_ref=ubuf.at[at, pl.ds(tokens, tokens), :],
            dst_ref=ubuf.at[at, pl.ds(0, tokens), :],
            send_sem=halo_send,
            recv_sem=halo_recv.at[c],
            device_id={"ctx": lax.rem(me + 1, n)},
            device_id_type=MESH,
        )

    for c in range(chunks):
        if c % (chunks // parts) == 0:
            for i in range(2):
                early(i, c // (chunks // parts)).wait()
        for b in range(c * per_chunk, (c + 1) * per_chunk):
            cols = pl.ds(b * LANES, LANES)
            ubuf[b, pl.ds(tokens, tokens), :] = (k_short[:, cols].astype(F32) * v_input[:, cols].astype(F32)).astype(BF16)
        if c == 0 and n > BLOCK:
            pl.semaphore_wait(barrier, n - 1)
        elif c == 0:
            ahead_of = jnp.logical_and(odd == 1, me < n - 1).astype(jnp.int32)
            pl.semaphore_wait(barrier, 1 + 2 * chip + ahead_of)

        @pl.when(me < n - 1)
        def _():
            halo(c).start()

    if n <= BLOCK:
        for step in range(1, chips):

            @pl.when(chip >= step)
            def _():
                for core in range(2):
                    signal(ready, me - odd - 2 * step + core)

    @pl.when(me == 0)
    def _():
        ubuf[:, pl.ds(0, tokens), :] = jnp.zeros((blocks, tokens, LANES), BF16)

    state[...] = jnp.zeros_like(state)

    for i in range(3):
        fetches[i].wait()
    rate = rates[...] * LOG2E
    scaled = weights[...] * jnp.sqrt(2.0 * rates[...])
    for i, x in enumerate((rate, scaled)):
        turned_modes[i] = jnp.transpose(jnp.concatenate([x, jnp.zeros((LANES - order, groups), F32)], 0))
    for i in range(2):
        row = turned_modes[i, pl.ds(0, blocks, stride=per), :]
        for g in range(1, per):
            row = row + pltpu.roll(turned_modes[i, pl.ds(g, blocks, stride=per), :], g * order, 1)
        modes[i] = row
    flip = (lax.rem(iota((tokens, tokens), 0) + iota((tokens, tokens), 1), tokens) == 0).astype(BF16)
    taps_t = jnp.transpose(taps[...].astype(F32)).astype(BF16)
    short_row[...] = jnp.dot(taps_t, flip, preferred_element_type=F32)

    lane = iota((order, LANES), 1)
    ahead = (lax.rem(lane, size) - size).astype(F32)
    first = lax.rem(lane, size) == 0
    first_row = lax.rem(iota((1, LANES), 1), size) == 0
    rows = -iota((size, LANES), 0).astype(F32)
    masks[0] = (iota((tap_rows, tokens), 0) < iota((tap_rows, tokens), 1)).astype(F32)
    masks[1] = (iota((tap_rows, tokens), 0) >= iota((tap_rows, tokens), 1)).astype(F32)
    long_mask[...] = (iota((size, LANES), 0) >= lax.rem(iota((size, LANES), 1), size)).astype(F32)
    def turn(row, count, shift):
        return pltpu.roll(jnp.broadcast_to(row, (count, LANES)), shift, 1, stride=1, stride_axis=0)

    def spread(x, start, count):
        at = start // LANES * LANES
        x = x[:, at : at + LANES]
        if x.shape[1] < LANES:
            x = jnp.concatenate([x, jnp.zeros((order, LANES - x.shape[1]), F32)], 1)
        return jnp.take_along_axis(x, start - at + lane // (LANES // count), axis=1)

    def make_tables(b):
        for g in range(per):
            turned = turn(short_row[pl.ds(b * per + g, 1), :], tap_rows, 0)
            for side in range(2):
                short_tab[b, side, pl.ds(g * tap_rows, tap_rows), :] = (turned * masks[side]).astype(BF16)
        for j in range(per // WINDOWS):
            start = b * per + j * WINDOWS
            table = jnp.exp2(spread(rate, start, WINDOWS) * ahead)
            hi, lo = split(table)
            long_tab[b, j, pl.ds(size, order), :] = hi
            long_tab[b, j, pl.ds(size + order, order), :] = lo
            row = jnp.sum(spread(scaled, start, WINDOWS) * jnp.where(first, 1.0, table), axis=0, keepdims=True)
            row = jnp.where(first_row, pltpu.roll(row, size, 1), row)
            long_tab[b, j, pl.ds(0, size), :] = (turn(row, size, LANES - size) * long_mask[...]).astype(BF16)
        lam_rc[:, pl.ds(b * LANES, LANES)] = spread(rate, b * per, per)
        out_tab[b] = (modes[1, pl.ds(b, 1), :] * jnp.exp2(modes[0, pl.ds(b, 1), :] * rows)).astype(BF16)

    lane_group = lax.rem(iota((tap_rows, SPANS * LANES), 1), LANES) // share
    lane_group_tall = lax.rem(iota((size, WINDOWS * LANES), 1), LANES) // share

    lane_group_order = lax.rem(iota((order, WINDOWS * LANES), 1), LANES) // share

    def stacked(x):
        return jnp.concatenate([x[:, i : i + LANES] for i in range(0, x.shape[1], LANES)], 0)

    def beside(x):
        return jnp.concatenate([x[i : i + size] for i in range(0, tokens, size)], 1)

    def short_blocks(bs):
        reach = tokens + tap_rows
        fulls = []
        for b in bs:
            spans = jnp.concatenate([ubuf[b, pl.ds(w * tap_rows, reach), :] for w in range(SPANS)], 1)
            table = jnp.concatenate([short_tab[b, 0], short_tab[b, 1][:, :tap_rows]], 1)
            fulls.append(jnp.dot(table, spans, preferred_element_type=F32))
        for b, full in zip(bs, fulls):
            cols = pl.ds(b * LANES, LANES)
            y = full[:tap_rows]
            for g in range(1, per):
                y = jnp.where(lane_group == g, full[g * tap_rows : (g + 1) * tap_rows], y)
            y = stacked(y)
            ulong[b] = (k_long[:, cols].astype(F32) * q_short[:, cols].astype(F32) * y).astype(BF16)

    def pieces(x):
        return [x[:, i : i + LANES] for i in range(0, x.shape[1], LANES)]

    def long_blocks(bs):
        for b in bs:
            cols = pl.ds(b * LANES, LANES)
            u = beside(ulong[b])
            tall = jnp.concatenate(
                [jnp.where(lane_group_tall == g, u, jnp.zeros_like(u)) for g in range(per)], 0
            )
            table = jnp.concatenate([long_tab[b, j] for j in range(per // WINDOWS)], 1)
            full = jnp.dot(table, tall, preferred_element_type=F32)
            ynear[b] = full[:size]
            local = full[size : size + order] + full[size + order :]
            inner[b] = local
            decay = jnp.exp2(-lam_rc[:, cols] * float(size))
            total = local[:, :LANES]
            for piece in pieces(local)[1:]:
                total = decay * total + piece
            plocal[:, cols] = total
            psend[0, :, cols] = total.astype(BF16)

    def final_blocks(bs):
        for b in bs:
            cols = pl.ds(b * LANES, LANES)
            decay = jnp.exp2(-lam_rc[:, cols] * float(size))
            starts = [state[:, cols]]
            for piece in pieces(inner[b])[:-1]:
                starts.append(decay * starts[-1] + piece)
            tall = jnp.concatenate(
                [
                    jnp.where(lane_group_order == g, x, jnp.zeros_like(x))
                    for x in split(jnp.concatenate(starts, 1))
                    for g in range(per)
                ],
                0,
            )
            table = out_tab[b]
            far = jnp.dot(jnp.concatenate([table, table], 1), tall, preferred_element_type=F32)
            y = stacked(ynear[b] + far).astype(BF16)
            out[:, cols] = (q_long[:, cols].astype(F32) * y.astype(F32)).astype(BF16)

    def members(c):
        return range(c * per_chunk, (c + 1) * per_chunk)

    def columns(g, to=None):
        start, stop = bounds[g][0] * width, bounds[g if to is None else to][1] * width
        return pl.ds(start, stop - start)

    def send(source, target, g, send_sem, device, to=None):
        cols = columns(g, to)
        return pltpu.make_async_remote_copy(
            src_ref=source.at[:, cols],
            dst_ref=precv.at[target, :, cols],
            send_sem=send_sem,
            recv_sem=scan_recv.at[target, g],
            device_id={"ctx": lax.rem(device, n)},
            device_id_type=MESH,
        )

    def swap(g, to=None):
        return send(psend.at[0], 0, g, swap_send, me + 1 - 2 * odd, to)

    def chip_copy(g, step, core, to=None):
        return send(psend.at[1], 1 + chip, g, chip_send.at[step - 1, core], me - odd + 2 * step + core, to)

    def forward(g, to=None):
        return send(precv.at[1], 1, g, forward_send, me + 1, to)

    def merged_copy(g, core, to=None):
        return send(psend.at[2], 2, g, merged_send.at[core], me + 4 + core, to)

    def block_copy(k, g, away, to=None):
        return send(psend.at[3], chips + k - first_level, g, block_send.at[away], me + 2 + away, to)

    def wait_arrival(slot, g):
        send(psend.at[0], slot, g, swap_send, me + 1).wait_recv()

    def received(slot, g):
        return precv[slot, :, columns(g)].astype(F32)

    def decayed(g, distance):
        return jnp.exp2(-lam_rc[:, columns(g)] * distance)

    end_chip = chips - 1
    inner_chip = jnp.logical_and(chip > 0, chip < end_chip)

    def odd_sends(g):
        return jnp.logical_and(odd == 1, chip < end_chip if g == 0 else chip == 0)

    def odd_swaps(g):
        swaps = inner_chip if g > 0 else chip == 1
        if n > BLOCK:
            swaps = jnp.logical_or(swaps, chip == end_chip)
        return jnp.logical_and(odd == 1, swaps)

    def own_total(g):
        return decayed(g, float(tokens)) * plocal[:, columns(g)] + received(0, g)

    def group_done(g):
        @pl.when(jnp.logical_or(odd == 0, odd_swaps(g)))
        def _():
            swap(g).start()

        if g > 0:

            @pl.when(jnp.logical_and(odd == 0, inner_chip))
            def _():
                wait_arrival(0, g)
                psend[1, :, columns(g)] = own_total(g).astype(BF16)
                for core in range(2):
                    chip_copy(g, 1, core).start()

    def odd_send(g):
        @pl.when(odd_sends(g))
        def _():
            wait_arrival(0, g)
            total = decayed(g, float(tokens)) * received(0, g) + plocal[:, columns(g)]
            psend[1, :, columns(g)] = total.astype(BF16)
            chip_copy(g, 1, 0).start()

            @pl.when(chip == 0)
            def _():
                chip_copy(g, 2, 0).start()

            if g == 0:

                @pl.when(chip > 0)
                def _():
                    chip_copy(g, 1, 1).start()

    def pass_first(g):
        @pl.when(jnp.logical_and(odd == 0, inner_chip))
        def _():
            wait_arrival(1, g)

        @pl.when(jnp.logical_and(odd == 0, chip == 1))
        def _():
            if g == 0:
                wait_arrival(0, g)
            total = decayed(g, float(2 * tokens)) * received(1, g) + own_total(g)
            psend[2, :, columns(g)] = total.astype(BF16)
            for core in range(2):
                merged_copy(g, core).start()

        @pl.when(jnp.logical_and(odd == 0, inner_chip))
        def _():
            forward(g).start()

    def take(g):
        cols = columns(g)
        for source in range(chips - 1):
            reached = inner_chip if source == 0 else chip > source

            @pl.when(jnp.logical_and(reached, odd == 1) if source == 0 else reached)
            def _():
                wait_arrival(1 + source, g)

            @pl.when(reached)
            def _():
                distance = ((chip - source - 1) * 2 + odd) * tokens
                state[:, cols] = state[:, cols] + decayed(g, distance.astype(F32)) * received(1 + source, g)

        @pl.when(jnp.logical_and(odd == 1, jnp.logical_not(odd_sends(g))))
        def _():
            wait_arrival(0, g)

        @pl.when(odd == 1)
        def _():
            state[:, cols] = state[:, cols] + received(0, g)

        if n > BLOCK:

            @pl.when(jnp.logical_and(odd == 0, chip == end_chip))
            def _():
                wait_arrival(0, g)

            for k in range(first_level, levels):

                @pl.when(lax.rem(me, 2 << k) >= 1 << k)
                def _():
                    distance = lax.rem(me, 1 << k) * tokens
                    slot = chips + k - first_level
                    wait_arrival(slot, g)
                    state[:, cols] = state[:, cols] + decayed(g, distance.astype(F32)) * received(slot, g)

                @pl.when(sends(k))
                def _():
                    total = decayed(g, float(2 * tokens)) * state[:, cols]
                    total = total + decayed(g, float(tokens)) * plocal[:, cols]
                    psend[3, :, cols] = (total + received(0, g)).astype(BF16)
                    for away in range(1 << k):
                        block_copy(k, g, away).start()

    def sends(k):
        return lax.rem(me, 2 << k) == (1 << k) - 2

    for b in members(0):
        make_tables(b)
    fetches[3].wait()
    fetches[4].wait()

    def after_long(c):
        for g, (_, stop) in enumerate(bounds):
            if stop == c + 1:
                group_done(g)

    for c in range(chunks):
        last = c == chunks - 1
        if c == chunks // 2 and n <= BLOCK:

            @pl.when(chip < chips - 1)
            def _():
                pl.semaphore_wait(ready, 2 * (chips - 1 - chip))

        if last and c > 0:
            long_blocks(members(c - 1))
            after_long(c - 1)

        @pl.when(me > 0)
        def _():
            halo(c).wait_recv()

        short_blocks(members(c))
        if not last:
            for b in members(c + 1):
                make_tables(b)
            if c > 0:
                long_blocks(members(c - 1))
                after_long(c - 1)

    long_blocks(members(chunks - 1))
    after_long(chunks - 1)
    for g in range(final + 1):
        odd_send(g)
    for g in range(final + 1):
        pass_first(g)
    fetches[5].wait()
    for g in range(final + 1):
        take(g)
        for c in range(*bounds[g]):
            final_blocks(members(c))

    @pl.when(me < n - 1)
    def _():
        halo(0, chunks).wait_send()

    @pl.when(odd == 0)
    def _():
        swap(0, final).wait_send()

    if n > BLOCK:

        @pl.when(jnp.logical_and(odd == 1, chip == end_chip))
        def _():
            swap(0, final).wait_send()

    for place, first in ((1, 0), (2, 1)):

        @pl.when(jnp.logical_and(odd == 1, chip == place))
        def _():
            swap(first, final).wait_send()

    @pl.when(jnp.logical_and(odd == 1, chip == 0))
    def _():
        for step in range(1, 3):
            chip_copy(0, step, 0, final).wait_send()

    @pl.when(inner_chip)
    def _():
        for core in range(2):

            @pl.when(odd == 1)
            def _():
                chip_copy(0, 1, core).wait_send()

            @pl.when(odd == 0)
            def _():
                chip_copy(1, 1, core, final).wait_send()

        @pl.when(odd == 0)
        def _():
            forward(0, final).wait_send()

    @pl.when(jnp.logical_and(odd == 0, chip == 1))
    def _():
        for core in range(2):
            merged_copy(0, core, final).wait_send()

    for k in range(first_level, levels):

        @pl.when(sends(k))
        def _():
            for away in range(1 << k):
                block_copy(k, 0, away, final).wait_send()


def on_device(n, *args):
    args = args[:6] + (args[6].T, args[7].T)
    args = tuple(pltpu.with_memory_space_constraint(a, pltpu.HBM) for a in args)
    q_short, taps, rates = args[0], args[5], args[6]
    tokens, ch = q_short.shape
    order, groups = rates.shape
    blocks = ch // LANES
    per = LANES * groups // ch
    chunks = max(c for c in (1, 2, 4, 8) if blocks % c == 0)
    levels = n.bit_length() - 1
    chips = min(n, BLOCK) // 2
    above = max(0, levels - chips.bit_length())
    dma = pltpu.SemaphoreType.DMA
    return pl.pallas_call(
        functools.partial(kernel, n, chunks),
        out_shape=jax.ShapeDtypeStruct((tokens, ch), BF16),
        in_specs=[pl.BlockSpec(memory_space=pltpu.HBM)] * 8,
        out_specs=pl.BlockSpec(memory_space=pltpu.VMEM),
        scratch_shapes=[
            pltpu.VMEM((tokens, ch), BF16),
            pltpu.VMEM((tokens, ch), BF16),
            pltpu.VMEM((tokens, ch), BF16),
            pltpu.VMEM((tokens, ch), BF16),
            pltpu.VMEM((tokens, ch), BF16),
            pltpu.VMEM(taps.shape, BF16),
            pltpu.VMEM((order, groups), F32),
            pltpu.VMEM((order, groups), F32),
            dma((6,)),
            dma((2, 2)),
            pltpu.VMEM((blocks, 2 * tokens, LANES), BF16),
            pltpu.VMEM((blocks, tokens, LANES), BF16),
            pltpu.VMEM((blocks, tokens // WINDOWS, WINDOWS * LANES), F32),
            pltpu.VMEM((blocks, 2, per * tokens // SPANS, tokens), BF16),
            pltpu.VMEM((blocks, per // WINDOWS, tokens // WINDOWS + 2 * order, LANES), BF16),
            pltpu.VMEM((blocks, tokens // WINDOWS, LANES), BF16),
            pltpu.VMEM((2, tokens // SPANS, tokens), F32),
            pltpu.VMEM((tokens // WINDOWS, LANES), F32),
            pltpu.VMEM((order, ch), F32),
            pltpu.VMEM((groups, tokens), F32),
            pltpu.VMEM((2, blocks, LANES), F32),
            pltpu.VMEM((2, groups, LANES), F32),
            pltpu.VMEM((order, ch), F32),
            pltpu.VMEM((blocks, order, WINDOWS * LANES), F32),
            pltpu.VMEM((order, ch), F32),
            pltpu.VMEM((4 if above else 3, order, ch), BF16),
            pltpu.VMEM((chips + above, order, ch), BF16),
            pltpu.SemaphoreType.REGULAR,
            dma,
            dma((chunks,)),
            dma,
            dma((2, 2)),
            dma,
            dma((2,)),
            dma((max(1, n // 2 if above else 1),)),
            dma((chips + above, 3)),
        ],
        compiler_params=pltpu.CompilerParams(
            collective_id=0, has_side_effects=True, vmem_limit_bytes=40 * 2**20
        ),
    )(*args)


def solution(mesh):
    in_specs = (P("ctx", "ch"),) * 5 + (P(None, "ch"), P("ch", None), P("ch", None))
    return jax.shard_map(
        functools.partial(on_device, mesh.shape["ctx"]),
        mesh=mesh,
        in_specs=in_specs,
        out_specs=P("ctx", "ch"),
        check_vma=False,
    )
```

```python
import functools
import math

import jax
import jax.numpy as jnp
from jax import lax
from jax.experimental import pallas as pl
from jax.experimental.pallas import tpu as pltpu
from jax.sharding import PartitionSpec as P

MESH = pl.DeviceIdType.MESH
LANES = 128
F32 = jnp.float32
BF16 = jnp.bfloat16
LOG2E = math.log2(math.e)
WINDOWS = 4
SPANS = 8
BLOCK = 8


def iota(shape, dim):
    return lax.broadcasted_iota(jnp.int32, shape, dim)


def split(x):
    hi = x.astype(BF16)
    return hi, (x - hi.astype(F32)).astype(BF16)


def kernel(
    n, chunks, q_short_in, k_short_in, v_input_in, q_long_in, k_long_in, taps_in, rates_in, weights_in, out,
    q_short, q_long, k_long, k_short, v_input, taps, rates, weights, fetch_sem, early_sem,
    ubuf, ulong, ynear, short_tab, long_tab, out_tab, masks, long_mask, lam_rc, short_row, modes,
    turned_modes, state, inner, plocal, psend, precv, ready, halo_send, halo_recv, swap_send, chip_send, forward_send, merged_send, block_send, scan_recv,
):
    me = lax.axis_index("ctx")
    tokens, ch = k_short.shape
    size = tokens // WINDOWS
    tap_rows = tokens // SPANS
    order, groups = rates.shape
    share = ch // groups
    per = LANES // share
    blocks = ch // LANES
    per_chunk = blocks // chunks
    width = per_chunk * LANES
    levels = n.bit_length() - 1
    chips = min(n, BLOCK) // 2
    odd = lax.rem(me, 2)
    chip = lax.rem(me, 2 * chips) // 2
    first_level = (2 * chips).bit_length() - 1
    bounds = sorted({chunks // 2, chunks - 1, chunks} - {0})
    bounds = list(zip([0] + bounds[:-1], bounds))
    final = len(bounds) - 1
    parts = 2 if chunks % 2 == 0 else 1

    def early(i, part):
        source, target = ((k_short_in, k_short), (v_input_in, v_input))[i]
        cols = pl.ds(part * (ch // parts), ch // parts)
        return pltpu.make_async_copy(source.at[:, cols], target.at[:, cols], early_sem.at[i, part])

    fetches = [
        pltpu.make_async_copy(source, target, fetch_sem.at[i])
        for i, (source, target) in enumerate(
            (
                (taps_in, taps),
                (rates_in, rates),
                (weights_in, weights),
                (k_long_in, k_long),
                (q_short_in, q_short),
                (q_long_in, q_long),
            )
        )
    ]
    barrier = pltpu.get_barrier_semaphore()

    def signal(semaphore, device):
        pl.semaphore_signal(
            semaphore, inc=1, device_id={"ctx": lax.rem(device + n, n)}, device_id_type=MESH
        )

    if n > BLOCK:
        for part in range(parts):
            for i in range(2):
                early(i, part).start()
        for step in range(1, n):
            signal(barrier, me + step)
    else:

        @pl.when(jnp.logical_and(odd == 0, me > 0))
        def _():
            signal(barrier, me - 1)

        for part in range(parts):
            for i in range(2):
                early(i, part).start()
        signal(barrier, me + 1 - 2 * odd)
        for step in range(1, chips):

            @pl.when(chip + step < chips)
            def _():
                for core in range(2):
                    signal(barrier, me - odd + 2 * step + core)

    for fetch in fetches:
        fetch.start()

    def halo(c, count=1):
        at = pl.ds(c * per_chunk, count * per_chunk)
        return pltpu.make_async_remote_copy(
            src_ref=ubuf.at[at, pl.ds(tokens, tokens), :],
            dst_ref=ubuf.at[at, pl.ds(0, tokens), :],
            send_sem=halo_send,
            recv_sem=halo_recv.at[c],
            device_id={"ctx": lax.rem(me + 1, n)},
            device_id_type=MESH,
        )

    for c in range(chunks):
        if c % (chunks // parts) == 0:
            for i in range(2):
                early(i, c // (chunks // parts)).wait()
        for b in range(c * per_chunk, (c + 1) * per_chunk):
            cols = pl.ds(b * LANES, LANES)
            ubuf[b, pl.ds(tokens, tokens), :] = (k_short[:, cols].astype(F32) * v_input[:, cols].astype(F32)).astype(BF16)
        if c == 0 and n > BLOCK:
            pl.semaphore_wait(barrier, n - 1)
        elif c == 0:
            ahead_of = jnp.logical_and(odd == 1, me < n - 1).astype(jnp.int32)
            pl.semaphore_wait(barrier, 1 + 2 * chip + ahead_of)

        @pl.when(me < n - 1)
        def _():
            halo(c).start()

    if n <= BLOCK:
        for step in range(1, chips):

            @pl.when(chip >= step)
            def _():
                for core in range(2):
                    signal(ready, me - odd - 2 * step + core)

    @pl.when(me == 0)
    def _():
        ubuf[:, pl.ds(0, tokens), :] = jnp.zeros((blocks, tokens, LANES), BF16)

    state[...] = jnp.zeros_like(state)

    for i in range(3):
        fetches[i].wait()
    rate = rates[...] * LOG2E
    scaled = weights[...] * jnp.sqrt(2.0 * rates[...])
    for i, x in enumerate((rate, scaled)):
        turned_modes[i] = jnp.transpose(jnp.concatenate([x, jnp.zeros((LANES - order, groups), F32)], 0))
    for i in range(2):
        row = turned_modes[i, pl.ds(0, blocks, stride=per), :]
        for g in range(1, per):
            row = row + pltpu.roll(turned_modes[i, pl.ds(g, blocks, stride=per), :], g * order, 1)
        modes[i] = row
    flip = (lax.rem(iota((tokens, tokens), 0) + iota((tokens, tokens), 1), tokens) == 0).astype(BF16)
    taps_t = jnp.transpose(taps[...].astype(F32)).astype(BF16)
    short_row[...] = jnp.dot(taps_t, flip, preferred_element_type=F32)

    lane = iota((order, LANES), 1)
    ahead = (lax.rem(lane, size) - size).astype(F32)
    first = lax.rem(lane, size) == 0
    first_row = lax.rem(iota((1, LANES), 1), size) == 0
    rows = -iota((tokens, LANES), 0).astype(F32)
    masks[0] = (iota((tap_rows, tokens), 0) < iota((tap_rows, tokens), 1)).astype(F32)
    masks[1] = (iota((tap_rows, tokens), 0) >= iota((tap_rows, tokens), 1)).astype(F32)
    long_mask[...] = (iota((size, LANES), 0) >= lax.rem(iota((size, LANES), 1), size)).astype(F32)
    def turn(row, count, shift):
        return pltpu.roll(jnp.broadcast_to(row, (count, LANES)), shift, 1, stride=1, stride_axis=0)

    def spread(x, start, count):
        at = start // LANES * LANES
        x = x[:, at : at + LANES]
        if x.shape[1] < LANES:
            x = jnp.concatenate([x, jnp.zeros((order, LANES - x.shape[1]), F32)], 1)
        return jnp.take_along_axis(x, start - at + lane // (LANES // count), axis=1)

    def make_tables(b):
        for g in range(per):
            turned = turn(short_row[pl.ds(b * per + g, 1), :], tap_rows, 0)
            for side in range(2):
                short_tab[b, side, pl.ds(g * tap_rows, tap_rows), :] = (turned * masks[side]).astype(BF16)
        for j in range(per // WINDOWS):
            start = b * per + j * WINDOWS
            table = jnp.exp2(spread(rate, start, WINDOWS) * ahead)
            hi, lo = split(table)
            long_tab[b, j, pl.ds(size, order), :] = hi
            long_tab[b, j, pl.ds(size + order, order), :] = lo
            row = jnp.sum(spread(scaled, start, WINDOWS) * jnp.where(first, 1.0, table), axis=0, keepdims=True)
            row = jnp.where(first_row, pltpu.roll(row, size, 1), row)
            long_tab[b, j, pl.ds(0, size), :] = (turn(row, size, LANES - size) * long_mask[...]).astype(BF16)
        lam_rc[:, pl.ds(b * LANES, LANES)] = spread(rate, b * per, per)
        out_tab[b] = (modes[1, pl.ds(b, 1), :] * jnp.exp2(modes[0, pl.ds(b, 1), :] * rows)).astype(BF16)

    lane_group = lax.rem(iota((tap_rows, SPANS * LANES), 1), LANES) // share
    lane_group_tall = lax.rem(iota((size, WINDOWS * LANES), 1), LANES) // share

    lane_group_order = lax.rem(iota((order, WINDOWS * LANES), 1), LANES) // share

    def stacked(x):
        return jnp.concatenate([x[:, i : i + LANES] for i in range(0, x.shape[1], LANES)], 0)

    def beside(x):
        return jnp.concatenate([x[i : i + size] for i in range(0, tokens, size)], 1)

    def short_blocks(bs):
        reach = tokens + tap_rows
        fulls = []
        for b in bs:
            spans = jnp.concatenate([ubuf[b, pl.ds(w * tap_rows, reach), :] for w in range(SPANS)], 1)
            table = jnp.concatenate([short_tab[b, 0], short_tab[b, 1][:, :tap_rows]], 1)
            fulls.append(jnp.dot(table, spans, preferred_element_type=F32))
        for b, full in zip(bs, fulls):
            cols = pl.ds(b * LANES, LANES)
            y = full[:tap_rows]
            for g in range(1, per):
                y = jnp.where(lane_group == g, full[g * tap_rows : (g + 1) * tap_rows], y)
            y = stacked(y)
            ulong[b] = (k_long[:, cols].astype(F32) * q_short[:, cols].astype(F32) * y).astype(BF16)

    def pieces(x):
        return [x[:, i : i + LANES] for i in range(0, x.shape[1], LANES)]

    def long_blocks(bs):
        for b in bs:
            cols = pl.ds(b * LANES, LANES)
            u = beside(ulong[b])
            tall = jnp.concatenate(
                [jnp.where(lane_group_tall == g, u, jnp.zeros_like(u)) for g in range(per)], 0
            )
            table = jnp.concatenate([long_tab[b, j] for j in range(per // WINDOWS)], 1)
            full = jnp.dot(table, tall, preferred_element_type=F32)
            ynear[b] = full[:size]
            local = full[size : size + order] + full[size + order :]
            inner[b] = local
            decay = jnp.exp2(-lam_rc[:, cols] * float(size))
            total = local[:, :LANES]
            for piece in pieces(local)[1:]:
                total = decay * total + piece
            plocal[:, cols] = total
            psend[0, :, cols] = total.astype(BF16)

    def expanded(x):
        group = lane_group_order[:, : x.shape[1]]
        return jnp.concatenate(
            [jnp.where(group == g, part, jnp.zeros_like(part)) for part in split(x) for g in range(per)], 0
        )

    def inner_blocks(bs):
        for b in bs:
            cols = pl.ds(b * LANES, LANES)
            decay = jnp.exp2(-lam_rc[:, cols] * float(size))
            sums = pieces(inner[b])[:-1]
            starts = [sums[0]]
            for piece in sums[1:]:
                starts.append(decay * starts[-1] + piece)
            table = out_tab[b, pl.ds(0, size), :]
            far = jnp.dot(
                jnp.concatenate([table, table], 1),
                expanded(jnp.concatenate(starts, 1)),
                preferred_element_type=F32,
            )
            ynear[b, :, pl.ds(LANES, (WINDOWS - 1) * LANES)] += far

    def final_blocks(bs):
        for b in bs:
            cols = pl.ds(b * LANES, LANES)
            table = out_tab[b]
            far = jnp.dot(
                jnp.concatenate([table, table], 1), expanded(state[:, cols]), preferred_element_type=F32
            )
            y = (stacked(ynear[b]) + far).astype(BF16)
            out[:, cols] = (q_long[:, cols].astype(F32) * y.astype(F32)).astype(BF16)

    def members(c):
        return range(c * per_chunk, (c + 1) * per_chunk)

    def columns(g, to=None):
        start, stop = bounds[g][0] * width, bounds[g if to is None else to][1] * width
        return pl.ds(start, stop - start)

    def send(source, target, g, send_sem, device, to=None):
        cols = columns(g, to)
        return pltpu.make_async_remote_copy(
            src_ref=source.at[:, cols],
            dst_ref=precv.at[target, :, cols],
            send_sem=send_sem,
            recv_sem=scan_recv.at[target, g],
            device_id={"ctx": lax.rem(device, n)},
            device_id_type=MESH,
        )

    def swap(g, to=None):
        return send(psend.at[0], 0, g, swap_send, me + 1 - 2 * odd, to)

    def chip_copy(g, step, core, to=None):
        return send(psend.at[1], 1 + chip, g, chip_send.at[step - 1, core], me - odd + 2 * step + core, to)

    def forward(g, to=None):
        return send(precv.at[1], 1, g, forward_send, me + 1, to)

    def merged_copy(g, core, to=None):
        return send(psend.at[2], 2, g, merged_send.at[core], me + 4 + core, to)

    def block_copy(k, g, away, to=None):
        return send(psend.at[3], chips + k - first_level, g, block_send.at[away], me + 2 + away, to)

    def wait_arrival(slot, g):
        send(psend.at[0], slot, g, swap_send, me + 1).wait_recv()

    def received(slot, g):
        return precv[slot, :, columns(g)].astype(F32)

    def decayed(g, distance):
        return jnp.exp2(-lam_rc[:, columns(g)] * distance)

    end_chip = chips - 1
    inner_chip = jnp.logical_and(chip > 0, chip < end_chip)

    def odd_sends(g):
        return jnp.logical_and(odd == 1, chip < end_chip if g == 0 else chip == 0)

    def odd_swaps(g):
        swaps = inner_chip if g > 0 else chip == 1
        if n > BLOCK:
            swaps = jnp.logical_or(swaps, chip == end_chip)
        return jnp.logical_and(odd == 1, swaps)

    def own_total(g):
        return decayed(g, float(tokens)) * plocal[:, columns(g)] + received(0, g)

    def group_done(g):
        @pl.when(jnp.logical_or(odd == 0, odd_swaps(g)))
        def _():
            swap(g).start()

        if g > 0:

            @pl.when(jnp.logical_and(odd == 0, inner_chip))
            def _():
                wait_arrival(0, g)
                psend[1, :, columns(g)] = own_total(g).astype(BF16)
                for core in range(2):
                    chip_copy(g, 1, core).start()

    def odd_send(g):
        @pl.when(odd_sends(g))
        def _():
            wait_arrival(0, g)
            total = decayed(g, float(tokens)) * received(0, g) + plocal[:, columns(g)]
            psend[1, :, columns(g)] = total.astype(BF16)
            chip_copy(g, 1, 0).start()

            @pl.when(chip == 0)
            def _():
                chip_copy(g, 2, 0).start()

            if g == 0:

                @pl.when(chip > 0)
                def _():
                    chip_copy(g, 1, 1).start()

    def pass_first(g):
        @pl.when(jnp.logical_and(odd == 0, inner_chip))
        def _():
            wait_arrival(1, g)

        @pl.when(jnp.logical_and(odd == 0, chip == 1))
        def _():
            if g == 0:
                wait_arrival(0, g)
            total = decayed(g, float(2 * tokens)) * received(1, g) + own_total(g)
            psend[2, :, columns(g)] = total.astype(BF16)
            for core in (1, 0):
                merged_copy(g, core).start()

        @pl.when(jnp.logical_and(odd == 0, inner_chip))
        def _():
            forward(g).start()

    def take(g):
        cols = columns(g)
        for source in range(chips - 1):
            reached = inner_chip if source == 0 else chip > source

            @pl.when(jnp.logical_and(reached, odd == 1) if source == 0 else reached)
            def _():
                wait_arrival(1 + source, g)

            @pl.when(reached)
            def _():
                distance = ((chip - source - 1) * 2 + odd) * tokens
                state[:, cols] = state[:, cols] + decayed(g, distance.astype(F32)) * received(1 + source, g)

        @pl.when(jnp.logical_and(odd == 1, jnp.logical_not(odd_sends(g))))
        def _():
            wait_arrival(0, g)

        @pl.when(odd == 1)
        def _():
            state[:, cols] = state[:, cols] + received(0, g)

        if n > BLOCK:

            @pl.when(jnp.logical_and(odd == 0, chip == end_chip))
            def _():
                wait_arrival(0, g)

            for k in range(first_level, levels):

                @pl.when(lax.rem(me, 2 << k) >= 1 << k)
                def _():
                    distance = lax.rem(me, 1 << k) * tokens
                    slot = chips + k - first_level
                    wait_arrival(slot, g)
                    state[:, cols] = state[:, cols] + decayed(g, distance.astype(F32)) * received(slot, g)

                @pl.when(sends(k))
                def _():
                    total = decayed(g, float(2 * tokens)) * state[:, cols]
                    total = total + decayed(g, float(tokens)) * plocal[:, cols]
                    psend[3, :, cols] = (total + received(0, g)).astype(BF16)
                    for away in range(1 << k):
                        block_copy(k, g, away).start()

    def sends(k):
        return lax.rem(me, 2 << k) == (1 << k) - 2

    for b in members(0):
        make_tables(b)
    fetches[3].wait()
    fetches[4].wait()

    def after_long(c):
        for g, (_, stop) in enumerate(bounds):
            if stop == c + 1:
                group_done(g)

    for c in range(chunks):
        last = c == chunks - 1
        if c == chunks // 2 and n <= BLOCK:

            @pl.when(chip < chips - 1)
            def _():
                pl.semaphore_wait(ready, 2 * (chips - 1 - chip))

        if last and c > 0:
            long_blocks(members(c - 1))
            after_long(c - 1)
            if c > 1:
                inner_blocks(members(c - 2))

        @pl.when(me > 0)
        def _():
            halo(c).wait_recv()

        short_blocks(members(c))
        if not last:
            for b in members(c + 1):
                make_tables(b)
            if c > 0:
                long_blocks(members(c - 1))
                if c > 1:
                    inner_blocks(members(c - 2))
                after_long(c - 1)

    long_blocks(members(chunks - 1))
    after_long(chunks - 1)
    for g in range(final + 1):
        odd_send(g)
    for g in range(final + 1):
        pass_first(g)
    for c in range(max(0, chunks - 2), chunks):
        inner_blocks(members(c))
    fetches[5].wait()
    for g in range(final + 1):
        take(g)
        for c in range(*bounds[g]):
            final_blocks(members(c))

    @pl.when(me < n - 1)
    def _():
        halo(0, chunks).wait_send()

    @pl.when(odd == 0)
    def _():
        swap(0, final).wait_send()

    if n > BLOCK:

        @pl.when(jnp.logical_and(odd == 1, chip == end_chip))
        def _():
            swap(0, final).wait_send()

    for place, first in ((1, 0), (2, 1)):

        @pl.when(jnp.logical_and(odd == 1, chip == place))
        def _():
            swap(first, final).wait_send()

    @pl.when(jnp.logical_and(odd == 1, chip == 0))
    def _():
        for step in range(1, 3):
            chip_copy(0, step, 0, final).wait_send()

    @pl.when(inner_chip)
    def _():
        for core in range(2):

            @pl.when(odd == 1)
            def _():
                chip_copy(0, 1, core).wait_send()

            @pl.when(odd == 0)
            def _():
                chip_copy(1, 1, core, final).wait_send()

        @pl.when(odd == 0)
        def _():
            forward(0, final).wait_send()

    @pl.when(jnp.logical_and(odd == 0, chip == 1))
    def _():
        for core in range(2):
            merged_copy(0, core, final).wait_send()

    for k in range(first_level, levels):

        @pl.when(sends(k))
        def _():
            for away in range(1 << k):
                block_copy(k, 0, away, final).wait_send()


def on_device(n, *args):
    args = args[:6] + (args[6].T, args[7].T)
    args = tuple(pltpu.with_memory_space_constraint(a, pltpu.HBM) for a in args)
    q_short, taps, rates = args[0], args[5], args[6]
    tokens, ch = q_short.shape
    order, groups = rates.shape
    blocks = ch // LANES
    per = LANES * groups // ch
    chunks = max(c for c in (1, 2, 4, 8) if blocks % c == 0)
    levels = n.bit_length() - 1
    chips = min(n, BLOCK) // 2
    above = max(0, levels - chips.bit_length())
    dma = pltpu.SemaphoreType.DMA
    return pl.pallas_call(
        functools.partial(kernel, n, chunks),
        out_shape=jax.ShapeDtypeStruct((tokens, ch), BF16),
        in_specs=[pl.BlockSpec(memory_space=pltpu.HBM)] * 8,
        out_specs=pl.BlockSpec(memory_space=pltpu.VMEM),
        scratch_shapes=[
            pltpu.VMEM((tokens, ch), BF16),
            pltpu.VMEM((tokens, ch), BF16),
            pltpu.VMEM((tokens, ch), BF16),
            pltpu.VMEM((tokens, ch), BF16),
            pltpu.VMEM((tokens, ch), BF16),
            pltpu.VMEM(taps.shape, BF16),
            pltpu.VMEM((order, groups), F32),
            pltpu.VMEM((order, groups), F32),
            dma((6,)),
            dma((2, 2)),
            pltpu.VMEM((blocks, 2 * tokens, LANES), BF16),
            pltpu.VMEM((blocks, tokens, LANES), BF16),
            pltpu.VMEM((blocks, tokens // WINDOWS, WINDOWS * LANES), F32),
            pltpu.VMEM((blocks, 2, per * tokens // SPANS, tokens), BF16),
            pltpu.VMEM((blocks, per // WINDOWS, tokens // WINDOWS + 2 * order, LANES), BF16),
            pltpu.VMEM((blocks, tokens, LANES), BF16),
            pltpu.VMEM((2, tokens // SPANS, tokens), F32),
            pltpu.VMEM((tokens // WINDOWS, LANES), F32),
            pltpu.VMEM((order, ch), F32),
            pltpu.VMEM((groups, tokens), F32),
            pltpu.VMEM((2, blocks, LANES), F32),
            pltpu.VMEM((2, groups, LANES), F32),
            pltpu.VMEM((order, ch), F32),
            pltpu.VMEM((blocks, order, WINDOWS * LANES), F32),
            pltpu.VMEM((order, ch), F32),
            pltpu.VMEM((4 if above else 3, order, ch), BF16),
            pltpu.VMEM((chips + above, order, ch), BF16),
            pltpu.SemaphoreType.REGULAR,
            dma,
            dma((chunks,)),
            dma,
            dma((2, 2)),
            dma,
            dma((2,)),
            dma((max(1, n // 2 if above else 1),)),
            dma((chips + above, 3)),
        ],
        compiler_params=pltpu.CompilerParams(
            collective_id=0, has_side_effects=True, vmem_limit_bytes=40 * 2**20
        ),
    )(*args)


def solution(mesh):
    in_specs = (P("ctx", "ch"),) * 5 + (P(None, "ch"), P("ch", None), P("ch", None))
    return jax.shard_map(
        functools.partial(on_device, mesh.shape["ctx"]),
        mesh=mesh,
        in_specs=in_specs,
        out_specs=P("ctx", "ch"),
        check_vma=False,
    )
```

```python
import functools
import math

import jax
import jax.numpy as jnp
from jax import lax
from jax.experimental import pallas as pl
from jax.experimental.pallas import tpu as pltpu
from jax.sharding import PartitionSpec as P

MESH = pl.DeviceIdType.MESH
LANES = 128
F32 = jnp.float32
BF16 = jnp.bfloat16
LOG2E = math.log2(math.e)
WINDOWS = 4
SPANS = 8
BLOCK = 8


def iota(shape, dim):
    return lax.broadcasted_iota(jnp.int32, shape, dim)


def split(x):
    hi = x.astype(BF16)
    return hi, (x - hi.astype(F32)).astype(BF16)


def kernel(
    n, chunks, q_short_in, k_short_in, v_input_in, q_long_in, k_long_in, taps_in, rates_in, weights_in, out,
    q_short, q_long, k_long, k_short, v_input, taps, rates, weights, fetch_sem, early_sem,
    ubuf, ulong, ynear, short_tab, long_tab, out_tab, masks, long_mask, lam_rc, short_row, modes,
    turned_modes, state, inner, plocal, psend, precv, ready, halo_send, halo_recv, swap_send, chip_send, forward_send, merged_send, block_send, scan_recv,
):
    me = lax.axis_index("ctx")
    tokens, ch = k_short.shape
    size = tokens // WINDOWS
    tap_rows = tokens // SPANS
    order, groups = rates.shape
    share = ch // groups
    per = LANES // share
    blocks = ch // LANES
    per_chunk = blocks // chunks
    width = per_chunk * LANES
    levels = n.bit_length() - 1
    chips = min(n, BLOCK) // 2
    odd = lax.rem(me, 2)
    chip = lax.rem(me, 2 * chips) // 2
    first_level = (2 * chips).bit_length() - 1
    bounds = sorted({chunks // 2, chunks - 1, chunks} - {0})
    bounds = list(zip([0] + bounds[:-1], bounds))
    final = len(bounds) - 1
    parts = 2 if chunks % 2 == 0 else 1

    def early(i, part):
        source, target = ((k_short_in, k_short), (v_input_in, v_input))[i]
        cols = pl.ds(part * (ch // parts), ch // parts)
        return pltpu.make_async_copy(source.at[:, cols], target.at[:, cols], early_sem.at[i, part])

    fetches = [
        pltpu.make_async_copy(source, target, fetch_sem.at[i])
        for i, (source, target) in enumerate(
            (
                (taps_in, taps),
                (rates_in, rates),
                (weights_in, weights),
                (k_long_in, k_long),
                (q_short_in, q_short),
                (q_long_in, q_long),
            )
        )
    ]
    barrier = pltpu.get_barrier_semaphore()

    def signal(semaphore, device):
        pl.semaphore_signal(
            semaphore, inc=1, device_id={"ctx": lax.rem(device + n, n)}, device_id_type=MESH
        )

    if n > BLOCK:
        for part in range(parts):
            for i in range(2):
                early(i, part).start()
        for step in range(1, n):
            signal(barrier, me + step)
    else:

        @pl.when(jnp.logical_and(odd == 0, me > 0))
        def _():
            signal(barrier, me - 1)

        for part in range(parts):
            for i in range(2):
                early(i, part).start()
        signal(barrier, me + 1 - 2 * odd)
        for step in range(1, chips):

            @pl.when(chip + step < chips)
            def _():
                for core in range(2):
                    signal(barrier, me - odd + 2 * step + core)

    for fetch in fetches:
        fetch.start()

    def halo(c, count=1):
        at = pl.ds(c * per_chunk, count * per_chunk)
        return pltpu.make_async_remote_copy(
            src_ref=ubuf.at[at, pl.ds(tokens, tokens), :],
            dst_ref=ubuf.at[at, pl.ds(0, tokens), :],
            send_sem=halo_send,
            recv_sem=halo_recv.at[c],
            device_id={"ctx": lax.rem(me + 1, n)},
            device_id_type=MESH,
        )

    for c in range(chunks):
        if c % (chunks // parts) == 0:
            for i in range(2):
                early(i, c // (chunks // parts)).wait()
        for b in range(c * per_chunk, (c + 1) * per_chunk):
            cols = pl.ds(b * LANES, LANES)
            ubuf[b, pl.ds(tokens, tokens), :] = (k_short[:, cols].astype(F32) * v_input[:, cols].astype(F32)).astype(BF16)
        if c == 0 and n > BLOCK:
            pl.semaphore_wait(barrier, n - 1)
        elif c == 0:
            ahead_of = jnp.logical_and(odd == 1, me < n - 1).astype(jnp.int32)
            pl.semaphore_wait(barrier, 1 + 2 * chip + ahead_of)

        @pl.when(me < n - 1)
        def _():
            halo(c).start()

    if n <= BLOCK:
        for step in range(1, chips):

            @pl.when(chip >= step)
            def _():
                for core in range(2):
                    signal(ready, me - odd - 2 * step + core)

    @pl.when(me == 0)
    def _():
        ubuf[:, pl.ds(0, tokens), :] = jnp.zeros((blocks, tokens, LANES), BF16)

    state[...] = jnp.zeros_like(state)

    for i in range(3):
        fetches[i].wait()
    rate = rates[...] * LOG2E
    scaled = weights[...] * jnp.sqrt(2.0 * rates[...])
    for i, x in enumerate((rate, scaled)):
        turned_modes[i] = jnp.transpose(jnp.concatenate([x, jnp.zeros((LANES - order, groups), F32)], 0))
    for i in range(2):
        row = turned_modes[i, pl.ds(0, blocks, stride=per), :]
        for g in range(1, per):
            row = row + pltpu.roll(turned_modes[i, pl.ds(g, blocks, stride=per), :], g * order, 1)
        modes[i] = row
    flip = (lax.rem(iota((tokens, tokens), 0) + iota((tokens, tokens), 1), tokens) == 0).astype(BF16)
    taps_t = jnp.transpose(taps[...].astype(F32)).astype(BF16)
    short_row[...] = jnp.dot(taps_t, flip, preferred_element_type=F32)

    lane = iota((order, LANES), 1)
    ahead = (lax.rem(lane, size) - size).astype(F32)
    first = lax.rem(lane, size) == 0
    first_row = lax.rem(iota((1, LANES), 1), size) == 0
    rows = -iota((tokens, LANES), 0).astype(F32)
    masks[0] = (iota((tap_rows, tokens), 0) < iota((tap_rows, tokens), 1)).astype(F32)
    masks[1] = (iota((tap_rows, tokens), 0) >= iota((tap_rows, tokens), 1)).astype(F32)
    long_mask[...] = (iota((size, LANES), 0) >= lax.rem(iota((size, LANES), 1), size)).astype(F32)
    def turn(row, count, shift):
        return pltpu.roll(jnp.broadcast_to(row, (count, LANES)), shift, 1, stride=1, stride_axis=0)

    def spread(x, start, count):
        at = start // LANES * LANES
        x = x[:, at : at + LANES]
        if x.shape[1] < LANES:
            x = jnp.concatenate([x, jnp.zeros((order, LANES - x.shape[1]), F32)], 1)
        return jnp.take_along_axis(x, start - at + lane // (LANES // count), axis=1)

    def make_tables(b):
        for g in range(per):
            turned = turn(short_row[pl.ds(b * per + g, 1), :], tap_rows, 0)
            for side in range(2):
                short_tab[b, side, pl.ds(g * tap_rows, tap_rows), :] = (turned * masks[side]).astype(BF16)
        for j in range(per // WINDOWS):
            start = b * per + j * WINDOWS
            table = jnp.exp2(spread(rate, start, WINDOWS) * ahead)
            hi, lo = split(table)
            long_tab[b, j, pl.ds(size, order), :] = hi
            long_tab[b, j, pl.ds(size + order, order), :] = lo
            row = jnp.sum(spread(scaled, start, WINDOWS) * jnp.where(first, 1.0, table), axis=0, keepdims=True)
            row = jnp.where(first_row, pltpu.roll(row, size, 1), row)
            long_tab[b, j, pl.ds(0, size), :] = (turn(row, size, LANES - size) * long_mask[...]).astype(BF16)
        lam_rc[:, pl.ds(b * LANES, LANES)] = spread(rate, b * per, per)
        out_tab[b] = (modes[1, pl.ds(b, 1), :] * jnp.exp2(modes[0, pl.ds(b, 1), :] * rows)).astype(BF16)

    lane_group = lax.rem(iota((tap_rows, SPANS * LANES), 1), LANES) // share
    lane_group_tall = lax.rem(iota((size, WINDOWS * LANES), 1), LANES) // share

    lane_group_order = lax.rem(iota((order, WINDOWS * LANES), 1), LANES) // share

    def stacked(x):
        return jnp.concatenate([x[:, i : i + LANES] for i in range(0, x.shape[1], LANES)], 0)

    def beside(x):
        return jnp.concatenate([x[i : i + size] for i in range(0, tokens, size)], 1)

    def short_blocks(bs):
        reach = tokens + tap_rows
        fulls = []
        for b in bs:
            spans = jnp.concatenate([ubuf[b, pl.ds(w * tap_rows, reach), :] for w in range(SPANS)], 1)
            table = jnp.concatenate([short_tab[b, 0], short_tab[b, 1][:, :tap_rows]], 1)
            fulls.append(jnp.dot(table, spans, preferred_element_type=F32))
        for b, full in zip(bs, fulls):
            cols = pl.ds(b * LANES, LANES)
            y = full[:tap_rows]
            for g in range(1, per):
                y = jnp.where(lane_group == g, full[g * tap_rows : (g + 1) * tap_rows], y)
            y = stacked(y)
            ulong[b] = (k_long[:, cols].astype(F32) * q_short[:, cols].astype(F32) * y).astype(BF16)

    def pieces(x):
        return [x[:, i : i + LANES] for i in range(0, x.shape[1], LANES)]

    def long_blocks(bs):
        for b in bs:
            cols = pl.ds(b * LANES, LANES)
            u = beside(ulong[b])
            tall = jnp.concatenate(
                [jnp.where(lane_group_tall == g, u, jnp.zeros_like(u)) for g in range(per)], 0
            )
            table = jnp.concatenate([long_tab[b, j] for j in range(per // WINDOWS)], 1)
            full = jnp.dot(table, tall, preferred_element_type=F32)
            ynear[b] = full[:size]
            local = full[size : size + order] + full[size + order :]
            inner[b] = local
            decay = jnp.exp2(-lam_rc[:, cols] * float(size))
            total = local[:, :LANES]
            for piece in pieces(local)[1:]:
                total = decay * total + piece
            plocal[:, cols] = total
            psend[0, :, cols] = total.astype(BF16)

    def expanded(x):
        group = lane_group_order[:, : x.shape[1]]
        return jnp.concatenate(
            [jnp.where(group == g, part, jnp.zeros_like(part)) for part in split(x) for g in range(per)], 0
        )

    def inner_blocks(bs):
        for b in bs:
            cols = pl.ds(b * LANES, LANES)
            decay = jnp.exp2(-lam_rc[:, cols] * float(size))
            sums = pieces(inner[b])[:-1]
            starts = [sums[0]]
            for piece in sums[1:]:
                starts.append(decay * starts[-1] + piece)
            table = out_tab[b, pl.ds(0, size), :]
            far = jnp.dot(
                jnp.concatenate([table, table], 1),
                expanded(jnp.concatenate(starts, 1)),
                preferred_element_type=F32,
            )
            ynear[b, :, pl.ds(LANES, (WINDOWS - 1) * LANES)] += far

    def final_blocks(bs):
        for b in bs:
            cols = pl.ds(b * LANES, LANES)
            table = out_tab[b]
            far = jnp.dot(
                jnp.concatenate([table, table], 1), expanded(state[:, cols]), preferred_element_type=F32
            )
            y = (stacked(ynear[b]) + far).astype(BF16)
            out[:, cols] = (q_long[:, cols].astype(F32) * y.astype(F32)).astype(BF16)

    def members(c):
        return range(c * per_chunk, (c + 1) * per_chunk)

    def columns(g, to=None):
        start, stop = bounds[g][0] * width, bounds[g if to is None else to][1] * width
        return pl.ds(start, stop - start)

    def send(source, target, g, send_sem, device, to=None):
        cols = columns(g, to)
        return pltpu.make_async_remote_copy(
            src_ref=source.at[:, cols],
            dst_ref=precv.at[target, :, cols],
            send_sem=send_sem,
            recv_sem=scan_recv.at[target, g],
            device_id={"ctx": lax.rem(device, n)},
            device_id_type=MESH,
        )

    def swap(g, to=None):
        return send(psend.at[0], 0, g, swap_send, me + 1 - 2 * odd, to)

    def chip_copy(g, step, core, to=None):
        return send(psend.at[1], 1 + chip, g, chip_send.at[step - 1, core], me - odd + 2 * step + core, to)

    def forward(g, to=None):
        return send(precv.at[1], 1, g, forward_send, me + 1, to)

    def merged_copy(g, core, to=None):
        return send(psend.at[2], 2, g, merged_send.at[core], me + 4 + core, to)

    def block_copy(k, g, away, to=None):
        return send(psend.at[3], chips + k - first_level, g, block_send.at[away], me + 2 + away, to)

    def wait_arrival(slot, g):
        send(psend.at[0], slot, g, swap_send, me + 1).wait_recv()

    def received(slot, g):
        return precv[slot, :, columns(g)].astype(F32)

    def decayed(g, distance):
        return jnp.exp2(-lam_rc[:, columns(g)] * distance)

    end_chip = chips - 1
    inner_chip = jnp.logical_and(chip > 0, chip < end_chip)

    def odd_sends(g):
        return jnp.logical_and(odd == 1, chip < end_chip if g == 0 else chip == 0)

    def odd_swaps(g):
        swaps = inner_chip if g > 0 else chip == 1
        if n > BLOCK:
            swaps = jnp.logical_or(swaps, chip == end_chip)
        return jnp.logical_and(odd == 1, swaps)

    def own_total(g):
        return decayed(g, float(tokens)) * plocal[:, columns(g)] + received(0, g)

    def group_done(g):
        @pl.when(jnp.logical_or(odd == 0, odd_swaps(g)))
        def _():
            swap(g).start()

        if g > 0:

            @pl.when(jnp.logical_and(odd == 0, inner_chip))
            def _():
                wait_arrival(0, g)
                psend[1, :, columns(g)] = own_total(g).astype(BF16)
                for core in range(2):
                    chip_copy(g, 1, core).start()

    def odd_send(g):
        @pl.when(odd_sends(g))
        def _():
            wait_arrival(0, g)
            total = decayed(g, float(tokens)) * received(0, g) + plocal[:, columns(g)]
            psend[1, :, columns(g)] = total.astype(BF16)
            chip_copy(g, 1, 0).start()

            @pl.when(chip == 0)
            def _():
                chip_copy(g, 2, 0).start()

            if g == 0:

                @pl.when(chip > 0)
                def _():
                    chip_copy(g, 1, 1).start()

    def merge(g):
        @pl.when(jnp.logical_and(odd == 0, chip == 1))
        def _():
            wait_arrival(1, g)
            if g == 0:
                wait_arrival(0, g)
            total = decayed(g, float(2 * tokens)) * received(1, g) + own_total(g)
            psend[2, :, columns(g)] = total.astype(BF16)
            for core in (1, 0):
                merged_copy(g, core).start()

    def pass_first(g):
        @pl.when(jnp.logical_and(odd == 0, chip == 2))
        def _():
            wait_arrival(1, g)

        @pl.when(jnp.logical_and(odd == 0, inner_chip))
        def _():
            forward(g).start()

    def take(g):
        cols = columns(g)
        for source in range(chips - 1):
            reached = inner_chip if source == 0 else chip > source

            @pl.when(jnp.logical_and(reached, odd == 1) if source == 0 else reached)
            def _():
                wait_arrival(1 + source, g)

            @pl.when(reached)
            def _():
                distance = ((chip - source - 1) * 2 + odd) * tokens
                state[:, cols] = state[:, cols] + decayed(g, distance.astype(F32)) * received(1 + source, g)

        @pl.when(jnp.logical_and(odd == 1, jnp.logical_not(odd_sends(g))))
        def _():
            wait_arrival(0, g)

        @pl.when(odd == 1)
        def _():
            state[:, cols] = state[:, cols] + received(0, g)

        if n > BLOCK:

            @pl.when(jnp.logical_and(odd == 0, chip == end_chip))
            def _():
                wait_arrival(0, g)

            for k in range(first_level, levels):

                @pl.when(lax.rem(me, 2 << k) >= 1 << k)
                def _():
                    distance = lax.rem(me, 1 << k) * tokens
                    slot = chips + k - first_level
                    wait_arrival(slot, g)
                    state[:, cols] = state[:, cols] + decayed(g, distance.astype(F32)) * received(slot, g)

                @pl.when(sends(k))
                def _():
                    total = decayed(g, float(2 * tokens)) * state[:, cols]
                    total = total + decayed(g, float(tokens)) * plocal[:, cols]
                    psend[3, :, cols] = (total + received(0, g)).astype(BF16)
                    for away in range(1 << k):
                        block_copy(k, g, away).start()

    def sends(k):
        return lax.rem(me, 2 << k) == (1 << k) - 2

    lead = max(1, chunks // 2)
    for c in range(lead):
        for b in members(c):
            make_tables(b)
    fetches[3].wait()
    fetches[4].wait()

    def after_long(c):
        for g, (_, stop) in enumerate(bounds):
            if stop == c + 1:
                group_done(g)

    for c in range(chunks):
        last = c == chunks - 1
        if c == chunks // 2 and n <= BLOCK:

            @pl.when(chip < chips - 1)
            def _():
                pl.semaphore_wait(ready, 2 * (chips - 1 - chip))

        if last and c > 0:
            long_blocks(members(c - 1))
            after_long(c - 1)

        @pl.when(me > 0)
        def _():
            halo(c).wait_recv()

        short_blocks(members(c))
        if not last:
            if c + lead < chunks:
                for b in members(c + lead):
                    make_tables(b)
            if c > 0:
                long_blocks(members(c - 1))
                if 1 < c < chunks - 2:
                    inner_blocks(members(c - 2))
                after_long(c - 1)

    merge(0)
    long_blocks(members(chunks - 1))
    after_long(chunks - 1)
    for g in range(final + 1):
        odd_send(g)
    for g in range(1, final + 1):
        merge(g)
    for g in range(final + 1):
        pass_first(g)
    for c in range(max(0, chunks - 4), chunks):
        inner_blocks(members(c))
    fetches[5].wait()
    for g in range(final + 1):
        take(g)
        for c in range(*bounds[g]):
            final_blocks(members(c))

    @pl.when(me < n - 1)
    def _():
        halo(0, chunks).wait_send()

    @pl.when(odd == 0)
    def _():
        swap(0, final).wait_send()

    if n > BLOCK:

        @pl.when(jnp.logical_and(odd == 1, chip == end_chip))
        def _():
            swap(0, final).wait_send()

    for place, first in ((1, 0), (2, 1)):

        @pl.when(jnp.logical_and(odd == 1, chip == place))
        def _():
            swap(first, final).wait_send()

    @pl.when(jnp.logical_and(odd == 1, chip == 0))
    def _():
        for step in range(1, 3):
            chip_copy(0, step, 0, final).wait_send()

    @pl.when(inner_chip)
    def _():
        for core in range(2):

            @pl.when(odd == 1)
            def _():
                chip_copy(0, 1, core).wait_send()

            @pl.when(odd == 0)
            def _():
                chip_copy(1, 1, core, final).wait_send()

        @pl.when(odd == 0)
        def _():
            forward(0, final).wait_send()

    @pl.when(jnp.logical_and(odd == 0, chip == 1))
    def _():
        for core in range(2):
            merged_copy(0, core, final).wait_send()

    for k in range(first_level, levels):

        @pl.when(sends(k))
        def _():
            for away in range(1 << k):
                block_copy(k, 0, away, final).wait_send()


def on_device(n, *args):
    args = args[:6] + (args[6].T, args[7].T)
    args = tuple(pltpu.with_memory_space_constraint(a, pltpu.HBM) for a in args)
    q_short, taps, rates = args[0], args[5], args[6]
    tokens, ch = q_short.shape
    order, groups = rates.shape
    blocks = ch // LANES
    per = LANES * groups // ch
    chunks = max(c for c in (1, 2, 4, 8) if blocks % c == 0)
    levels = n.bit_length() - 1
    chips = min(n, BLOCK) // 2
    above = max(0, levels - chips.bit_length())
    dma = pltpu.SemaphoreType.DMA
    return pl.pallas_call(
        functools.partial(kernel, n, chunks),
        out_shape=jax.ShapeDtypeStruct((tokens, ch), BF16),
        in_specs=[pl.BlockSpec(memory_space=pltpu.HBM)] * 8,
        out_specs=pl.BlockSpec(memory_space=pltpu.VMEM),
        scratch_shapes=[
            pltpu.VMEM((tokens, ch), BF16),
            pltpu.VMEM((tokens, ch), BF16),
            pltpu.VMEM((tokens, ch), BF16),
            pltpu.VMEM((tokens, ch), BF16),
            pltpu.VMEM((tokens, ch), BF16),
            pltpu.VMEM(taps.shape, BF16),
            pltpu.VMEM((order, groups), F32),
            pltpu.VMEM((order, groups), F32),
            dma((6,)),
            dma((2, 2)),
            pltpu.VMEM((blocks, 2 * tokens, LANES), BF16),
            pltpu.VMEM((blocks, tokens, LANES), BF16),
            pltpu.VMEM((blocks, tokens // WINDOWS, WINDOWS * LANES), F32),
            pltpu.VMEM((blocks, 2, per * tokens // SPANS, tokens), BF16),
            pltpu.VMEM((blocks, per // WINDOWS, tokens // WINDOWS + 2 * order, LANES), BF16),
            pltpu.VMEM((blocks, tokens, LANES), BF16),
            pltpu.VMEM((2, tokens // SPANS, tokens), F32),
            pltpu.VMEM((tokens // WINDOWS, LANES), F32),
            pltpu.VMEM((order, ch), F32),
            pltpu.VMEM((groups, tokens), F32),
            pltpu.VMEM((2, blocks, LANES), F32),
            pltpu.VMEM((2, groups, LANES), F32),
            pltpu.VMEM((order, ch), F32),
            pltpu.VMEM((blocks, order, WINDOWS * LANES), F32),
            pltpu.VMEM((order, ch), F32),
            pltpu.VMEM((4 if above else 3, order, ch), BF16),
            pltpu.VMEM((chips + above, order, ch), BF16),
            pltpu.SemaphoreType.REGULAR,
            dma,
            dma((chunks,)),
            dma,
            dma((2, 2)),
            dma,
            dma((2,)),
            dma((max(1, n // 2 if above else 1),)),
            dma((chips + above, 3)),
        ],
        compiler_params=pltpu.CompilerParams(
            collective_id=0, has_side_effects=True, vmem_limit_bytes=40 * 2**20
        ),
    )(*args)


def solution(mesh):
    in_specs = (P("ctx", "ch"),) * 5 + (P(None, "ch"), P("ch", None), P("ch", None))
    return jax.shard_map(
        functools.partial(on_device, mesh.shape["ctx"]),
        mesh=mesh,
        in_specs=in_specs,
        out_specs=P("ctx", "ch"),
        check_vma=False,
    )
```

```python
import functools
import math

import jax
import jax.numpy as jnp
from jax import lax
from jax.experimental import pallas as pl
from jax.experimental.pallas import tpu as pltpu
from jax.sharding import PartitionSpec as P

MESH = pl.DeviceIdType.MESH
LANES = 128
F32 = jnp.float32
BF16 = jnp.bfloat16
LOG2E = math.log2(math.e)
WINDOWS = 4
SPANS = 8
BLOCK = 8


def iota(shape, dim):
    return lax.broadcasted_iota(jnp.int32, shape, dim)


def split(x):
    hi = x.astype(BF16)
    return hi, (x - hi.astype(F32)).astype(BF16)


def kernel(
    n, chunks, q_short_in, k_short_in, v_input_in, q_long_in, k_long_in, taps_in, rates_in, weights_in, out,
    q_short, q_long, k_long, k_short, v_input, taps, rates, weights, fetch_sem, early_sem,
    ubuf, ulong, ynear, short_tab, long_tab, out_tab, masks, long_mask, lam_rc, short_row, modes,
    turned_modes, state, inner, plocal, psend, precv, ready, halo_send, halo_recv, swap_send, chip_send, forward_send, merged_send, block_send, scan_recv,
):
    me = lax.axis_index("ctx")
    tokens, ch = k_short.shape
    size = tokens // WINDOWS
    tap_rows = tokens // SPANS
    order, groups = rates.shape
    share = ch // groups
    per = LANES // share
    blocks = ch // LANES
    per_chunk = blocks // chunks
    width = per_chunk * LANES
    levels = n.bit_length() - 1
    chips = min(n, BLOCK) // 2
    odd = lax.rem(me, 2)
    chip = lax.rem(me, 2 * chips) // 2
    first_level = (2 * chips).bit_length() - 1
    bounds = sorted({chunks // 2, chunks - 1, chunks} - {0})
    bounds = list(zip([0] + bounds[:-1], bounds))
    final = len(bounds) - 1
    parts = 2 if chunks % 2 == 0 else 1

    def early(i, part):
        source, target = ((k_short_in, k_short), (v_input_in, v_input))[i]
        cols = pl.ds(part * (ch // parts), ch // parts)
        return pltpu.make_async_copy(source.at[:, cols], target.at[:, cols], early_sem.at[i, part])

    fetches = [
        pltpu.make_async_copy(source, target, fetch_sem.at[i])
        for i, (source, target) in enumerate(
            (
                (taps_in, taps),
                (rates_in, rates),
                (weights_in, weights),
                (k_long_in, k_long),
                (q_short_in, q_short),
                (q_long_in, q_long),
            )
        )
    ]
    barrier = pltpu.get_barrier_semaphore()

    def signal(semaphore, device):
        pl.semaphore_signal(
            semaphore, inc=1, device_id={"ctx": lax.rem(device + n, n)}, device_id_type=MESH
        )

    if n > BLOCK:
        for part in range(parts):
            for i in range(2):
                early(i, part).start()
        for step in range(1, n):
            signal(barrier, me + step)
    else:

        @pl.when(jnp.logical_and(odd == 0, me > 0))
        def _():
            signal(barrier, me - 1)

        for part in range(parts):
            for i in range(2):
                early(i, part).start()
        signal(barrier, me + 1 - 2 * odd)
        for step in range(1, chips):

            @pl.when(chip + step < chips)
            def _():
                for core in range(2):
                    signal(barrier, me - odd + 2 * step + core)

    for fetch in fetches:
        fetch.start()

    def halo(c, count=1):
        at = pl.ds(c * per_chunk, count * per_chunk)
        return pltpu.make_async_remote_copy(
            src_ref=ubuf.at[at, pl.ds(tokens, tokens), :],
            dst_ref=ubuf.at[at, pl.ds(0, tokens), :],
            send_sem=halo_send,
            recv_sem=halo_recv.at[c],
            device_id={"ctx": lax.rem(me + 1, n)},
            device_id_type=MESH,
        )

    for c in range(chunks):
        if c % (chunks // parts) == 0:
            for i in range(2):
                early(i, c // (chunks // parts)).wait()
        for b in range(c * per_chunk, (c + 1) * per_chunk):
            cols = pl.ds(b * LANES, LANES)
            ubuf[b, pl.ds(tokens, tokens), :] = (k_short[:, cols].astype(F32) * v_input[:, cols].astype(F32)).astype(BF16)
        if c == 0 and n > BLOCK:
            pl.semaphore_wait(barrier, n - 1)
        elif c == 0:
            ahead_of = jnp.logical_and(odd == 1, me < n - 1).astype(jnp.int32)
            pl.semaphore_wait(barrier, 1 + 2 * chip + ahead_of)

        @pl.when(me < n - 1)
        def _():
            halo(c).start()

    if n <= BLOCK:
        for step in range(1, chips):

            @pl.when(chip >= step)
            def _():
                for core in range(2):
                    signal(ready, me - odd - 2 * step + core)

    @pl.when(me == 0)
    def _():
        ubuf[:, pl.ds(0, tokens), :] = jnp.zeros((blocks, tokens, LANES), BF16)

    state[...] = jnp.zeros_like(state)

    for i in range(3):
        fetches[i].wait()
    rate = rates[...] * LOG2E
    scaled = weights[...] * jnp.sqrt(2.0 * rates[...])
    for i, x in enumerate((rate, scaled)):
        turned_modes[i] = jnp.transpose(jnp.concatenate([x, jnp.zeros((LANES - order, groups), F32)], 0))
    for i in range(2):
        row = turned_modes[i, pl.ds(0, blocks, stride=per), :]
        for g in range(1, per):
            row = row + pltpu.roll(turned_modes[i, pl.ds(g, blocks, stride=per), :], g * order, 1)
        modes[i] = row
    flip = (lax.rem(iota((tokens, tokens), 0) + iota((tokens, tokens), 1), tokens) == 0).astype(BF16)
    taps_t = jnp.transpose(taps[...].astype(F32)).astype(BF16)
    short_row[...] = jnp.dot(taps_t, flip, preferred_element_type=F32)

    lane = iota((order, LANES), 1)
    ahead = (lax.rem(lane, size) - size).astype(F32)
    first = lax.rem(lane, size) == 0
    first_row = lax.rem(iota((1, LANES), 1), size) == 0
    rows = -iota((tokens, LANES), 0).astype(F32)
    masks[0] = (iota((tap_rows, tokens), 0) < iota((tap_rows, tokens), 1)).astype(F32)
    masks[1] = (iota((tap_rows, tokens), 0) >= iota((tap_rows, tokens), 1)).astype(F32)
    long_mask[...] = (iota((size, LANES), 0) >= lax.rem(iota((size, LANES), 1), size)).astype(F32)
    def turn(row, count, shift):
        return pltpu.roll(jnp.broadcast_to(row, (count, LANES)), shift, 1, stride=1, stride_axis=0)

    def spread(x, start, count):
        at = start // LANES * LANES
        x = x[:, at : at + LANES]
        if x.shape[1] < LANES:
            x = jnp.concatenate([x, jnp.zeros((order, LANES - x.shape[1]), F32)], 1)
        return jnp.take_along_axis(x, start - at + lane // (LANES // count), axis=1)

    def make_tables(b):
        for g in range(per):
            turned = turn(short_row[pl.ds(b * per + g, 1), :], tap_rows, 0)
            for side in range(2):
                short_tab[b, side, pl.ds(g * tap_rows, tap_rows), :] = (turned * masks[side]).astype(BF16)
        for j in range(per // WINDOWS):
            start = b * per + j * WINDOWS
            table = jnp.exp2(spread(rate, start, WINDOWS) * ahead)
            hi, lo = split(table)
            long_tab[b, j, pl.ds(size, order), :] = hi
            long_tab[b, j, pl.ds(size + order, order), :] = lo
            row = jnp.sum(spread(scaled, start, WINDOWS) * jnp.where(first, 1.0, table), axis=0, keepdims=True)
            row = jnp.where(first_row, pltpu.roll(row, size, 1), row)
            long_tab[b, j, pl.ds(0, size), :] = (turn(row, size, LANES - size) * long_mask[...]).astype(BF16)
        lam_rc[:, pl.ds(b * LANES, LANES)] = spread(rate, b * per, per)
        out_tab[b] = (modes[1, pl.ds(b, 1), :] * jnp.exp2(modes[0, pl.ds(b, 1), :] * rows)).astype(BF16)

    lane_group = lax.rem(iota((tap_rows, SPANS * LANES), 1), LANES) // share
    lane_group_tall = lax.rem(iota((size, WINDOWS * LANES), 1), LANES) // share

    lane_group_order = lax.rem(iota((order, WINDOWS * LANES), 1), LANES) // share

    def stacked(x):
        return jnp.concatenate([x[:, i : i + LANES] for i in range(0, x.shape[1], LANES)], 0)

    def beside(x):
        return jnp.concatenate([x[i : i + size] for i in range(0, tokens, size)], 1)

    def short_blocks(bs):
        reach = tokens + tap_rows
        fulls = []
        for b in bs:
            spans = jnp.concatenate([ubuf[b, pl.ds(w * tap_rows, reach), :] for w in range(SPANS)], 1)
            table = jnp.concatenate([short_tab[b, 0], short_tab[b, 1][:, :tap_rows]], 1)
            fulls.append(jnp.dot(table, spans, preferred_element_type=F32))
        for b, full in zip(bs, fulls):
            cols = pl.ds(b * LANES, LANES)
            y = full[:tap_rows]
            for g in range(1, per):
                y = jnp.where(lane_group == g, full[g * tap_rows : (g + 1) * tap_rows], y)
            y = stacked(y)
            ulong[b] = (k_long[:, cols].astype(F32) * q_short[:, cols].astype(F32) * y).astype(BF16)

    def pieces(x):
        return [x[:, i : i + LANES] for i in range(0, x.shape[1], LANES)]

    def long_blocks(bs):
        for b in bs:
            cols = pl.ds(b * LANES, LANES)
            u = beside(ulong[b])
            tall = jnp.concatenate(
                [jnp.where(lane_group_tall == g, u, jnp.zeros_like(u)) for g in range(per)], 0
            )
            table = jnp.concatenate([long_tab[b, j] for j in range(per // WINDOWS)], 1)
            full = jnp.dot(table, tall, preferred_element_type=F32)
            ynear[b] = full[:size]
            local = full[size : size + order] + full[size + order :]
            inner[b] = local
            decay = jnp.exp2(-lam_rc[:, cols] * float(size))
            total = local[:, :LANES]
            for piece in pieces(local)[1:]:
                total = decay * total + piece
            plocal[:, cols] = total
            psend[0, :, cols] = total.astype(BF16)

    def expanded(x):
        group = lane_group_order[:, : x.shape[1]]
        return jnp.concatenate(
            [jnp.where(group == g, part, jnp.zeros_like(part)) for part in split(x) for g in range(per)], 0
        )

    def inner_blocks(bs):
        for b in bs:
            cols = pl.ds(b * LANES, LANES)
            decay = jnp.exp2(-lam_rc[:, cols] * float(size))
            sums = pieces(inner[b])[:-1]
            starts = [sums[0]]
            for piece in sums[1:]:
                starts.append(decay * starts[-1] + piece)
            table = out_tab[b, pl.ds(0, size), :]
            far = jnp.dot(
                jnp.concatenate([table, table], 1),
                expanded(jnp.concatenate(starts, 1)),
                preferred_element_type=F32,
            )
            ynear[b, :, pl.ds(LANES, (WINDOWS - 1) * LANES)] += far

    def final_blocks(bs):
        for b in bs:
            cols = pl.ds(b * LANES, LANES)
            table = out_tab[b]
            far = jnp.dot(
                jnp.concatenate([table, table], 1), expanded(state[:, cols]), preferred_element_type=F32
            )
            y = (stacked(ynear[b]) + far).astype(BF16)
            out[:, cols] = (q_long[:, cols].astype(F32) * y.astype(F32)).astype(BF16)

    def members(c):
        return range(c * per_chunk, (c + 1) * per_chunk)

    def columns(g, to=None):
        start, stop = bounds[g][0] * width, bounds[g if to is None else to][1] * width
        return pl.ds(start, stop - start)

    def send(source, target, g, send_sem, device, to=None):
        cols = columns(g, to)
        return pltpu.make_async_remote_copy(
            src_ref=source.at[:, cols],
            dst_ref=precv.at[target, :, cols],
            send_sem=send_sem,
            recv_sem=scan_recv.at[target, g],
            device_id={"ctx": lax.rem(device, n)},
            device_id_type=MESH,
        )

    def swap(g, to=None):
        return send(psend.at[0], 0, g, swap_send, me + 1 - 2 * odd, to)

    def chip_copy(g, step, core, to=None):
        return send(psend.at[1], 1 + chip, g, chip_send.at[step - 1, core], me - odd + 2 * step + core, to)

    def forward(g, to=None):
        return send(precv.at[1], 1, g, forward_send, me + 1, to)

    def merged_copy(g, core, to=None):
        return send(psend.at[2], 2, g, merged_send.at[core], me + 4 + core, to)

    def block_copy(k, g, away, to=None):
        return send(psend.at[3], chips + k - first_level, g, block_send.at[away], me + 2 + away, to)

    def wait_arrival(slot, g):
        send(psend.at[0], slot, g, swap_send, me + 1).wait_recv()

    def received(slot, g):
        return precv[slot, :, columns(g)].astype(F32)

    def decayed(g, distance):
        return jnp.exp2(-lam_rc[:, columns(g)] * distance)

    end_chip = chips - 1
    inner_chip = jnp.logical_and(chip > 0, chip < end_chip)

    def odd_sends(g):
        return jnp.logical_and(odd == 1, chip < end_chip if g == 0 else chip == 0)

    def odd_swaps(g):
        swaps = inner_chip if g > 0 else chip == 1
        if n > BLOCK:
            swaps = jnp.logical_or(swaps, chip == end_chip)
        return jnp.logical_and(odd == 1, swaps)

    def own_total(g):
        return decayed(g, float(tokens)) * plocal[:, columns(g)] + received(0, g)

    def group_done(g):
        @pl.when(jnp.logical_or(odd == 0, odd_swaps(g)))
        def _():
            swap(g).start()

        if g > 0:

            @pl.when(jnp.logical_and(odd == 0, inner_chip))
            def _():
                wait_arrival(0, g)
                psend[1, :, columns(g)] = own_total(g).astype(BF16)
                for core in range(2):
                    chip_copy(g, 1, core).start()

    def odd_send(g):
        @pl.when(odd_sends(g))
        def _():
            wait_arrival(0, g)
            total = decayed(g, float(tokens)) * received(0, g) + plocal[:, columns(g)]
            psend[1, :, columns(g)] = total.astype(BF16)
            chip_copy(g, 1, 0).start()

            @pl.when(chip == 0)
            def _():
                chip_copy(g, 2, 0).start()

            if g == 0:

                @pl.when(chip > 0)
                def _():
                    chip_copy(g, 1, 1).start()

    def merge(g):
        @pl.when(jnp.logical_and(odd == 0, chip == 1))
        def _():
            wait_arrival(1, g)
            if g == 0:
                wait_arrival(0, g)
            total = decayed(g, float(2 * tokens)) * received(1, g) + own_total(g)
            psend[2, :, columns(g)] = total.astype(BF16)
            for core in (1, 0):
                merged_copy(g, core).start()

    def pass_first(g):
        @pl.when(jnp.logical_and(odd == 0, chip == 2))
        def _():
            wait_arrival(1, g)

        @pl.when(jnp.logical_and(odd == 0, inner_chip))
        def _():
            forward(g).start()

    def take(g):
        cols = columns(g)
        for source in range(chips - 1):
            reached = inner_chip if source == 0 else chip > source

            @pl.when(jnp.logical_and(reached, odd == 1) if source == 0 else reached)
            def _():
                wait_arrival(1 + source, g)

            @pl.when(reached)
            def _():
                distance = ((chip - source - 1) * 2 + odd) * tokens
                state[:, cols] = state[:, cols] + decayed(g, distance.astype(F32)) * received(1 + source, g)

        @pl.when(jnp.logical_and(odd == 1, jnp.logical_not(odd_sends(g))))
        def _():
            wait_arrival(0, g)

        @pl.when(odd == 1)
        def _():
            state[:, cols] = state[:, cols] + received(0, g)

        if n > BLOCK:

            @pl.when(jnp.logical_and(odd == 0, chip == end_chip))
            def _():
                wait_arrival(0, g)

            for k in range(first_level, levels):

                @pl.when(lax.rem(me, 2 << k) >= 1 << k)
                def _():
                    distance = lax.rem(me, 1 << k) * tokens
                    slot = chips + k - first_level
                    wait_arrival(slot, g)
                    state[:, cols] = state[:, cols] + decayed(g, distance.astype(F32)) * received(slot, g)

                @pl.when(sends(k))
                def _():
                    total = decayed(g, float(2 * tokens)) * state[:, cols]
                    total = total + decayed(g, float(tokens)) * plocal[:, cols]
                    psend[3, :, cols] = (total + received(0, g)).astype(BF16)
                    for away in range(1 << k):
                        block_copy(k, g, away).start()

    def sends(k):
        return lax.rem(me, 2 << k) == (1 << k) - 2

    lead = max(1, chunks // 4)
    for c in range(lead):
        for b in members(c):
            make_tables(b)
    fetches[3].wait()
    fetches[4].wait()

    def after_long(c):
        for g, (_, stop) in enumerate(bounds):
            if stop == c + 1:
                group_done(g)

    for c in range(chunks):
        last = c == chunks - 1
        if c == chunks // 2 and n <= BLOCK:

            @pl.when(chip < chips - 1)
            def _():
                pl.semaphore_wait(ready, 2 * (chips - 1 - chip))

        if last and c > 0:
            long_blocks(members(c - 1))
            after_long(c - 1)

        @pl.when(me > 0)
        def _():
            halo(c).wait_recv()

        short_blocks(members(c))
        if not last:
            if c + lead < chunks:
                for b in members(c + lead):
                    make_tables(b)
            if c > 0:
                long_blocks(members(c - 1))
                if 1 < c < chunks - 2:
                    inner_blocks(members(c - 2))
                after_long(c - 1)

    merge(0)
    long_blocks(members(chunks - 1))
    after_long(chunks - 1)
    for g in range(final + 1):
        odd_send(g)
    for g in range(1, final + 1):
        merge(g)
    for g in range(final + 1):
        pass_first(g)
    for c in range(max(0, chunks - 4), chunks):
        inner_blocks(members(c))
    fetches[5].wait()
    for g in range(final + 1):
        take(g)
        for c in range(*bounds[g]):
            final_blocks(members(c))

    @pl.when(me < n - 1)
    def _():
        halo(0, chunks).wait_send()

    @pl.when(odd == 0)
    def _():
        swap(0, final).wait_send()

    if n > BLOCK:

        @pl.when(jnp.logical_and(odd == 1, chip == end_chip))
        def _():
            swap(0, final).wait_send()

    for place, first in ((1, 0), (2, 1)):

        @pl.when(jnp.logical_and(odd == 1, chip == place))
        def _():
            swap(first, final).wait_send()

    @pl.when(jnp.logical_and(odd == 1, chip == 0))
    def _():
        for step in range(1, 3):
            chip_copy(0, step, 0, final).wait_send()

    @pl.when(inner_chip)
    def _():
        for core in range(2):

            @pl.when(odd == 1)
            def _():
                chip_copy(0, 1, core).wait_send()

            @pl.when(odd == 0)
            def _():
                chip_copy(1, 1, core, final).wait_send()

        @pl.when(odd == 0)
        def _():
            forward(0, final).wait_send()

    @pl.when(jnp.logical_and(odd == 0, chip == 1))
    def _():
        for core in range(2):
            merged_copy(0, core, final).wait_send()

    for k in range(first_level, levels):

        @pl.when(sends(k))
        def _():
            for away in range(1 << k):
                block_copy(k, 0, away, final).wait_send()


def on_device(n, *args):
    args = args[:6] + (args[6].T, args[7].T)
    args = tuple(pltpu.with_memory_space_constraint(a, pltpu.HBM) for a in args)
    q_short, taps, rates = args[0], args[5], args[6]
    tokens, ch = q_short.shape
    order, groups = rates.shape
    blocks = ch // LANES
    per = LANES * groups // ch
    chunks = max(c for c in (1, 2, 4, 8) if blocks % c == 0)
    levels = n.bit_length() - 1
    chips = min(n, BLOCK) // 2
    above = max(0, levels - chips.bit_length())
    dma = pltpu.SemaphoreType.DMA
    return pl.pallas_call(
        functools.partial(kernel, n, chunks),
        out_shape=jax.ShapeDtypeStruct((tokens, ch), BF16),
        in_specs=[pl.BlockSpec(memory_space=pltpu.HBM)] * 8,
        out_specs=pl.BlockSpec(memory_space=pltpu.VMEM),
        scratch_shapes=[
            pltpu.VMEM((tokens, ch), BF16),
            pltpu.VMEM((tokens, ch), BF16),
            pltpu.VMEM((tokens, ch), BF16),
            pltpu.VMEM((tokens, ch), BF16),
            pltpu.VMEM((tokens, ch), BF16),
            pltpu.VMEM(taps.shape, BF16),
            pltpu.VMEM((order, groups), F32),
            pltpu.VMEM((order, groups), F32),
            dma((6,)),
            dma((2, 2)),
            pltpu.VMEM((blocks, 2 * tokens, LANES), BF16),
            pltpu.VMEM((blocks, tokens, LANES), BF16),
            pltpu.VMEM((blocks, tokens // WINDOWS, WINDOWS * LANES), F32),
            pltpu.VMEM((blocks, 2, per * tokens // SPANS, tokens), BF16),
            pltpu.VMEM((blocks, per // WINDOWS, tokens // WINDOWS + 2 * order, LANES), BF16),
            pltpu.VMEM((blocks, tokens, LANES), BF16),
            pltpu.VMEM((2, tokens // SPANS, tokens), F32),
            pltpu.VMEM((tokens // WINDOWS, LANES), F32),
            pltpu.VMEM((order, ch), F32),
            pltpu.VMEM((groups, tokens), F32),
            pltpu.VMEM((2, blocks, LANES), F32),
            pltpu.VMEM((2, groups, LANES), F32),
            pltpu.VMEM((order, ch), F32),
            pltpu.VMEM((blocks, order, WINDOWS * LANES), F32),
            pltpu.VMEM((order, ch), F32),
            pltpu.VMEM((4 if above else 3, order, ch), BF16),
            pltpu.VMEM((chips + above, order, ch), BF16),
            pltpu.SemaphoreType.REGULAR,
            dma,
            dma((chunks,)),
            dma,
            dma((2, 2)),
            dma,
            dma((2,)),
            dma((max(1, n // 2 if above else 1),)),
            dma((chips + above, 3)),
        ],
        compiler_params=pltpu.CompilerParams(
            collective_id=0, has_side_effects=True, vmem_limit_bytes=40 * 2**20
        ),
    )(*args)


def solution(mesh):
    in_specs = (P("ctx", "ch"),) * 5 + (P(None, "ch"), P("ch", None), P("ch", None))
    return jax.shard_map(
        functools.partial(on_device, mesh.shape["ctx"]),
        mesh=mesh,
        in_specs=in_specs,
        out_specs=P("ctx", "ch"),
        check_vma=False,
    )
```
